32 devices in a mesh: face: 4 (over z), strip: 8 (over y, x, core).
Axes of the slice: x: 2, y: 2, z: 4, core: 2. Of those that a mesh axis runs over, the one named last changes fastest.
Arguments:
- pixels_in: bfloat16 [4, 8, 64, 1024], P('face', 'strip'), may hold values from -6 to 6
- w_qkv: bfloat16 [1024, 3072], P(None, 'face'), may hold values from -0.1875 to 0.1875
- w_gate: bfloat16 [1024, 32], P(None, 'face'), may hold values from -0.1875 to 0.1875
- decay_rate: float32 [16], replicated, may hold values from 0.0005859375 to 0.05
- beta_bias: float32 [16], replicated, may hold values from -4 to 1
Outputs:
- mixed: bfloat16 [4, 8, 64, 1024], P('face', 'strip')
The draws below stay inside these ranges and needn't reach their ends.
All inputs are finite; a program needn't handle non-finite values.
Results may differ from the reference program's by a relative error of at most 0.0069.
Values may be sent and summed in bfloat16 or wider, within the bound.
A program may use at most 192 MiB of HBM per device.

```python
import math
import jax
import jax.numpy as jnp
from jax import lax

D = 1024
H = 16
DK = 64
FACE_ROWS = 8
FACE_COLS = 64
FACES = 4
HV = 1024


def shard_levels(rng, shape, shards, low, top_value):
    gain, own = 1.0, jax.random.fold_in(rng, 6)
    for dim, blocks in shards:
        heights = jnp.exp(jax.random.uniform(jax.random.fold_in(own, dim), (blocks,), jnp.float32, low / len(shards), top_value / len(shards)))
        gain = gain * jnp.repeat(heights, shape[dim] // blocks).reshape([-1 if axis == dim else 1 for axis in range(len(shape))])
    return gain


def gaussian(key, dims, scale, most, split=(), kind=jnp.bfloat16):
    values = scale * jax.random.normal(key, dims, jnp.float32)
    if split:
        values = values * shard_levels(key, dims, split, -0.22, 0.18)
    return jnp.clip(values, -most, most).astype(kind)


def setup_inputs(seed: int = 0) -> dict:
    key_of = jax.random.split(jax.random.key(seed), 6)
    pixels_in = gaussian(key_of[0], (FACES, FACE_ROWS, FACE_COLS, D), 1.0, 6.0, ((0, 4), (1, 8)))
    w_qkv = gaussian(key_of[1], (D, 3 * H * DK), D ** -0.5, 0.1875, ((1, 4),))
    w_gate = gaussian(key_of[2], (D, 2 * H), D ** -0.5, 0.1875, ((1, 4),))
    decay_rate = jnp.clip(jnp.exp(jax.random.uniform(key_of[3], (H,), jnp.float32, math.log(0.0005859375), math.log(0.05))), 0.0005859375, 0.05)
    beta_bias = jnp.clip(jax.random.uniform(key_of[4], (H,), jnp.float32, -4.0, 1.0), -4.0, 1.0)
    return dict(pixels_in=pixels_in, w_qkv=w_qkv, w_gate=w_gate, decay_rate=decay_rate, beta_bias=beta_bias)


highest = lax.Precision.HIGHEST

def unit_rows(tensor):
    return tensor / jnp.sqrt(lax.optimization_barrier(jnp.sum(tensor * tensor, axis=-1, keepdims=True)) + 1e-06)

def head_norm(tensor):
    normed = tensor / jnp.sqrt(lax.optimization_barrier(jnp.mean(tensor * tensor, axis=-1, keepdims=True)) + 1e-06)
    return normed.reshape(tensor.shape[0], -1)

def project(flat_px, w_qkv, w_gate):
    projected = jnp.dot(flat_px.astype(jnp.float32), w_qkv.astype(jnp.float32), preferred_element_type=jnp.float32).astype(jnp.bfloat16)
    gate_logits = jnp.dot(flat_px.astype(jnp.float32), w_gate.astype(jnp.float32), preferred_element_type=jnp.float32).astype(jnp.bfloat16)
    return (projected, gate_logits)

def unpack(projected, gate_logits, decay_rate, beta_bias):
    heads = decay_rate.shape[0]
    count = projected.shape[0]
    parts = projected.astype(jnp.float32).reshape(count, 3, heads, -1)
    logits = gate_logits.astype(jnp.float32)
    log_decay = -decay_rate[None, :] * jnp.exp(logits[:, :heads])
    strength = jax.nn.sigmoid(logits[:, heads:] + beta_bias[None, :])
    return (unit_rows(parts[:, 0]), unit_rows(parts[:, 1]), parts[:, 2], log_decay, strength)

def group_terms(queries, key_rows, val_rows, log_decay, strength):
    span = queries.shape[1]
    width = queries.shape[2]
    cumulative = jnp.cumsum(log_decay, axis=1)
    gap_log = cumulative[:, :, None] - cumulative[:, None, :]
    row_ids = lax.broadcasted_iota(jnp.int32, (span, span), 0)
    col_ids = lax.broadcasted_iota(jnp.int32, (span, span), 1)
    inclusive = row_ids >= col_ids
    strict = row_ids > col_ids
    within = jnp.where(inclusive, jnp.exp(jnp.where(inclusive, gap_log, 0.0)), 0.0)
    key_dot = jnp.einsum('hck,hjk->hcj', key_rows, key_rows, precision=highest)
    lower_part = jnp.where(strict, within * key_dot, 0.0) * strength[:, :, None]
    system = lower_part + jnp.eye(span, dtype=queries.dtype)
    scale_all = jnp.exp(cumulative)
    rhs_values = val_rows * strength[:, :, None]
    rhs_keys = key_rows * (strength * scale_all)[:, :, None]
    solved = lax.linalg.triangular_solve(system, jnp.concatenate([rhs_values, rhs_keys], axis=-1), left_side=True, lower=True, unit_diagonal=True)
    new_values = solved[..., :width]
    mixing = solved[..., width:]
    scores = jnp.where(inclusive, within * jnp.einsum('hck,hjk->hcj', queries, key_rows, precision=highest), 0.0)
    tail_decay = jnp.exp(cumulative[:, -1:] - cumulative)
    weighted_keys = key_rows * tail_decay[:, :, None]
    end_scale = jnp.exp(cumulative[:, -1])
    transition = end_scale[:, None, None] * jnp.eye(width, dtype=queries.dtype) - jnp.einsum('hck,hcj->hkj', mixing, weighted_keys, precision=highest)
    writes = jnp.einsum('hcv,hck->hvk', new_values, weighted_keys, precision=highest)
    effective_query = queries * scale_all[:, :, None] - jnp.einsum('hcj,hjk->hck', scores, mixing, precision=highest)
    local_out = jnp.einsum('hcj,hjv->hcv', scores, new_values, precision=highest)
    return (local_out, effective_query, transition, writes)

def to_blocks(queries, key_rows, val_rows, log_decay, strength):
    count = queries.shape[0] // 64

    def shape_four(tensor):
        return tensor.reshape(count, 64, tensor.shape[1], tensor.shape[2]).transpose(0, 2, 1, 3)

    def shape_three(tensor):
        return tensor.reshape(count, 64, tensor.shape[1]).transpose(0, 2, 1)
    return (shape_four(queries), shape_four(key_rows), shape_four(val_rows), shape_three(log_decay), shape_three(strength))

def from_blocks(outputs):
    count, heads, span, width = outputs.shape
    return outputs.transpose(0, 2, 1, 3).reshape(count * span, heads, width)

def sequence_scan(queries, key_rows, val_rows, log_decay, strength):
    blocks = to_blocks(queries, key_rows, val_rows, log_decay, strength)
    heads = queries.shape[1]
    width = queries.shape[2]

    def advance(carry_state, block_in):
        local_out, effective_query, transition, writes = group_terms(*block_in)
        outputs = local_out + jnp.einsum('hck,hvk->hcv', effective_query, carry_state, precision=highest)
        carry_state = jnp.einsum('hvk,hkj->hvj', carry_state, transition, precision=highest) + writes
        return (carry_state, outputs)
    start = jnp.zeros((heads, width, width), queries.dtype)
    _, outputs = lax.scan(advance, start, blocks)
    return from_blocks(outputs)

def reference(pixels_in, w_qkv, w_gate, decay_rate, beta_bias):

    def column_order(tensor):
        rest = tensor.shape[1:]
        return tensor.reshape((FACE_ROWS, FACE_COLS) + rest).swapaxes(0, 1).reshape((FACE_ROWS * FACE_COLS,) + rest)

    def one_face(face_px):
        flat_px = face_px.reshape(FACE_ROWS * FACE_COLS, D)
        projected, gate_logits = project(flat_px, w_qkv, w_gate)
        unpacked = unpack(projected, gate_logits, decay_rate, beta_bias)
        row_out = sequence_scan(*unpacked)
        col_out = sequence_scan(*[column_order(tensor) for tensor in unpacked])
        col_mixed = head_norm(col_out).astype(jnp.bfloat16)
        col_rowwise = col_mixed.reshape(FACE_COLS, FACE_ROWS, HV).swapaxes(0, 1).reshape(FACE_ROWS * FACE_COLS, HV)
        mixed = (head_norm(row_out) + col_rowwise.astype(jnp.float32)).astype(jnp.bfloat16)
        return mixed.reshape(FACE_ROWS, FACE_COLS, HV)
    return lax.map(one_face, pixels_in)
```

```python
import functools

import jax
import jax.numpy as jnp
from jax import lax
from jax.experimental import pallas as pl
from jax.experimental.pallas import tpu as pltpu
from jax.sharding import PartitionSpec as P

MESH = pl.DeviceIdType.MESH
f32 = jnp.float32
bf16 = jnp.bfloat16


def greet_all(faces, strips, me_f, me_s):
    barrier = pltpu.get_barrier_semaphore()
    total = faces * strips
    me = me_f * strips + me_s

    def one(step, carry):
        other = lax.rem(me + step, total)
        pl.semaphore_signal(
            barrier,
            inc=1,
            device_id=(other // strips, lax.rem(other, strips)),
            device_id_type=MESH,
        )
        return carry

    lax.fori_loop(1, total, one, 0)
    pl.semaphore_wait(barrier, total - 1)


def project_kernel(
    cfg, px_ref, wq_ref, wg_ref, slabs_ref, gates_ref,
    px_all, proj, glog, px_send, px_recv, slab_send, slab_recv, gate_send, gate_recv,
):
    faces, strips, groups, rep, heads, per_group = cfg
    me_f, me_s = lax.axis_index("face"), lax.axis_index("strip")
    n_slab = proj.shape[1]
    gate_cols = wg_ref.shape[1]
    width = proj.shape[3]
    n_gate = gate_cols // per_group
    greet_all(faces, strips, me_f, me_s)

    def px_copy(step):
        face = lax.rem(me_f + step, faces)
        return pltpu.make_async_remote_copy(
            src_ref=px_ref,
            dst_ref=px_all.at[me_f],
            send_sem=px_send.at[step],
            recv_sem=px_recv.at[me_f],
            device_id=(face, me_s),
            device_id_type=MESH,
        )

    for step in range(1, faces):
        px_copy(step).start()

    def slab_copy(step, j, r):
        face = lax.rem(me_f + step, faces)
        slab = me_f * n_slab + j
        kind, group = slab // groups, lax.rem(slab, groups)
        dest = group * rep + r
        remote = pltpu.make_async_remote_copy(
            src_ref=proj.at[step, j],
            dst_ref=slabs_ref.at[kind, me_s],
            send_sem=slab_send.at[step, j, r],
            recv_sem=slab_recv.at[kind, me_s],
            device_id=(face, dest),
            device_id_type=MESH,
        )
        local = pltpu.make_async_copy(
            proj.at[step, j], slabs_ref.at[kind, me_s], slab_recv.at[kind, me_s]
        )
        return remote, local, dest

    def gate_copy(step, i, r):
        face = lax.rem(me_f + step, faces)
        first = me_f * gate_cols
        kind, group = first // heads, lax.rem(first, heads) // per_group + i
        dest = group * rep + r
        remote = pltpu.make_async_remote_copy(
            src_ref=glog.at[step],
            dst_ref=gates_ref.at[kind, me_s],
            send_sem=gate_send.at[step, i, r],
            recv_sem=gate_recv.at[kind, me_s],
            device_id=(face, dest),
            device_id_type=MESH,
        )
        local = pltpu.make_async_copy(
            glog.at[step], gates_ref.at[kind, me_s], gate_recv.at[kind, me_s]
        )
        return remote, local, dest

    def launch(copies, step):
        remote, local, dest = copies
        if step == 0:
            pl.when(dest == me_s)(local.start)
            pl.when(dest != me_s)(remote.start)
        else:
            remote.start()

    def drain(copies, step):
        remote, _, dest = copies
        if step == 0:
            pl.when(dest != me_s)(remote.wait_send)
        else:
            remote.wait_send()

    for step in range(faces):
        if step == 0:
            px = px_ref[...]
        else:
            face = lax.rem(me_f + step, faces)
            pltpu.make_async_copy(px_ref, px_all.at[face], px_recv.at[face]).wait()
            px = px_all[face]
        logits = jnp.dot(px, wg_ref[...], preferred_element_type=f32)
        glog[step] = logits.astype(bf16).astype(f32).T
        for i in range(n_gate):
            for r in range(rep):
                launch(gate_copy(step, i, r), step)
        for j in range(n_slab):
            proj[step, j] = jnp.dot(
                px, wq_ref[:, j * width : (j + 1) * width], preferred_element_type=f32
            ).astype(bf16)
        for j in range(n_slab):
            for r in range(rep):
                launch(slab_copy(step, j, r), step)

    for step in range(1, faces):
        px_copy(step).wait_send()
    for step in range(faces):
        for i in range(n_gate):
            for r in range(rep):
                drain(gate_copy(step, i, r), step)
        for j in range(n_slab):
            for r in range(rep):
                drain(slab_copy(step, j, r), step)
    for source in range(strips):
        for kind in range(slabs_ref.shape[0]):
            pltpu.make_async_copy(
                proj.at[0, 0], slabs_ref.at[kind, source], slab_recv.at[kind, source]
            ).wait()
        for kind in range(gates_ref.shape[0]):
            pltpu.make_async_copy(
                glog.at[0], gates_ref.at[kind, source], gate_recv.at[kind, source]
            ).wait()


def mm(a, b, dims=((1,), (0,))):
    return lax.dot_general(
        a.astype(bf16), b.astype(bf16), (dims, ((), ())), preferred_element_type=f32
    )


def split_mm(exact, wide, pieces):
    exact = exact.astype(bf16)
    total, rest = None, wide
    for _ in range(pieces):
        piece = rest.astype(bf16)
        rest = rest - piece.astype(f32)
        term = jnp.dot(exact, piece, preferred_element_type=f32)
        total = term if total is None else total + term
    return total


def mm_split(wide, exact, pieces):
    exact = exact.astype(bf16)
    total, rest = None, wide
    for _ in range(pieces):
        piece = rest.astype(bf16)
        rest = rest - piece.astype(f32)
        term = jnp.dot(piece, exact, preferred_element_type=f32)
        total = term if total is None else total + term
    return total


def scan_kernel(
    cfg, first_ref, slabs_ref, gates_ref, rate_ref, bias_ref, out_ref,
    feats, gates, row_buf, col_buf, states,
):
    chunk, per_group, tall, wide, dk = cfg
    strips, block, width = slabs_ref.shape[1:]
    count = strips * block
    first = first_ref[0]
    gate_cols = gates_ref.shape[2]

    lane = lax.broadcasted_iota(jnp.int32, (width, width), 1)
    sub = lax.broadcasted_iota(jnp.int32, (width, width), 0)
    same_head = (lane // dk) == (sub // dk)
    head_ones = same_head.astype(f32)
    ti = lax.broadcasted_iota(jnp.int32, (chunk, chunk), 0)
    tj = lax.broadcasted_iota(jnp.int32, (chunk, chunk), 1)
    inclusive = ti >= tj
    tri = inclusive.astype(f32)
    eye = (ti == tj).astype(f32)

    def prepare(s, carry):
        at = pl.ds(s * block, block)
        for kind in range(3):
            x = slabs_ref[kind, s].astype(f32)
            if kind < 2:
                x = x * lax.rsqrt(mm_split(x * x, head_ones, 2) + 1e-06)
            feats[kind, at, :] = x
        for a in range(per_group):
            head = first + a
            row = lax.rem(head, gate_cols)
            decay = -rate_ref[head] * jnp.exp(gates_ref[0, s, pl.ds(row, 1), :])
            strength = jax.nn.sigmoid(gates_ref[1, s, pl.ds(row, 1), :] + bias_ref[head])
            gates[a, at, :] = jnp.broadcast_to(decay, (chunk, block)).T
            gates[per_group + a, at, :] = jnp.broadcast_to(strength, (chunk, block)).T
        return carry

    lax.fori_loop(0, strips, prepare, 0, unroll=True if strips <= 8 else 1)

    columns = chunk // tall
    flane = lax.broadcasted_iota(jnp.int32, (chunk, width), 1) // dk

    def lanes_of(parts):
        out = parts[0][:, :width]
        for a in range(1, per_group):
            out = jnp.where(flane == a, parts[a][:, :width], out)
        return out

    def stacked(x):
        if per_group == 1:
            return x
        return jnp.concatenate(
            [jnp.where(flane == a, x, jnp.zeros_like(x)) for a in range(per_group)], axis=0
        )

    def side_by_side(parts):
        return parts[0] if per_group == 1 else jnp.concatenate(parts, axis=1)

    def load(ref, which, i, by_column):
        if not by_column:
            return ref[which, pl.ds(pl.multiple_of(i * chunk, chunk), chunk), :]
        return jnp.concatenate(
            [ref[which, pl.ds(i * columns + c, tall, stride=wide), :] for c in range(columns)],
            axis=0,
        )

    states[...] = jnp.zeros_like(states)

    def advance(i, carry):
        work = []
        for order in range(2):
            q, k, v = (load(feats, kind, i, order) for kind in range(3))
            cums, betas, systems, scores = [], [], [], []
            for a in range(per_group):
                cum = split_mm(tri, load(gates, a, i, order), 3)
                beta = load(gates, per_group + a, i, order)
                gap = cum - cum.T
                within = jnp.where(inclusive, jnp.exp(jnp.where(inclusive, gap, 0.0)), 0.0)
                k_a = k if per_group == 1 else jnp.where(flane == a, k, 0.0)
                q_a = q if per_group == 1 else jnp.where(flane == a, q, 0.0)
                dots = mm(jnp.concatenate([k_a, q_a], axis=0), k, ((1,), (1,)))
                systems.append(within * dots[:chunk] * beta)
                scores.append(within * dots[chunk:])
                cums.append(cum)
                betas.append(beta)
            work.append((q, k, v, cums, betas, systems, scores))

        inverses = [[None] * per_group for _ in range(2)]
        half = 1
        while half < chunk:
            here = ((ti // (2 * half)) == (tj // (2 * half))) & (
                (lax.rem(ti, 2 * half) >= half) & (lax.rem(tj, 2 * half) < half)
            )
            lows = [
                [jnp.where(here, work[o][5][a], 0.0) for a in range(per_group)] for o in range(2)
            ]
            if half == 1:
                inverses = [[eye - low for low in row] for row in lows]
            else:
                firsts = [
                    [mm(lows[o][a], inverses[o][a]) for a in range(per_group)] for o in range(2)
                ]
                inverses = [
                    [inverses[o][a] - mm(inverses[o][a], firsts[o][a]) for a in range(per_group)]
                    for o in range(2)
                ]
            half *= 2

        for order in range(2):
            q, k, v, cums, betas, _, scores = work[order]
            beta = lanes_of(betas)
            cum = lanes_of(cums)
            scale = jnp.exp(cum)
            last = cum[chunk - 1 : chunk, :]
            tail = jnp.exp(last - cum)
            both = side_by_side(inverses[order])
            u = mm(both, stacked(v * beta))
            w = mm(both, stacked(k * (beta * scale)))
            state = states[order]
            fresh = u - mm(w, state)
            out = mm(q * scale, state) + mm(side_by_side(scores), stacked(fresh))
            grown = mm(k * tail, fresh, ((0,), (0,)))
            decayed = state * jnp.exp(last)
            states[order] = decayed + jnp.where(same_head, grown, 0.0)
            normed = out * lax.rsqrt(mm_split(out * out, head_ones, 2) * (1.0 / dk) + 1e-06)
            if order == 0:
                row_buf[pl.ds(pl.multiple_of(i * chunk, chunk), chunk), :] = normed
            else:
                normed = normed.astype(bf16).astype(f32)
                for c in range(columns):
                    col_buf[pl.ds(i * columns + c, tall, stride=wide), :] = normed[
                        c * tall : (c + 1) * tall
                    ]
        return carry

    lax.fori_loop(0, count // chunk, advance, 0)

    def finish(s, carry):
        at = pl.ds(s * block, block)
        out_ref[s] = (row_buf[at, :] + col_buf[at, :]).astype(bf16)
        return carry

    lax.fori_loop(0, strips, finish, 0)


def return_kernel(faces, strips, mixed_ref, out_ref, send_sem, recv_sem):
    me_f, me_s = lax.axis_index("face"), lax.axis_index("strip")
    barrier = pltpu.get_barrier_semaphore()
    for step in range(1, strips):
        pl.semaphore_signal(
            barrier, inc=1, device_id=(me_f, lax.rem(me_s + step, strips)), device_id_type=MESH
        )
    pl.semaphore_wait(barrier, strips - 1)

    def copy(step):
        dest = lax.rem(me_s + step, strips)
        return pltpu.make_async_remote_copy(
            src_ref=mixed_ref.at[dest],
            dst_ref=out_ref.at[me_s],
            send_sem=send_sem.at[step],
            recv_sem=recv_sem.at[me_s],
            device_id=(me_f, dest),
            device_id_type=MESH,
        )

    for step in range(1, strips):
        copy(step).start()
    own = pltpu.make_async_copy(mixed_ref.at[me_s], out_ref.at[me_s], recv_sem.at[me_s])
    own.start()
    for step in range(1, strips):
        copy(step).wait_send()
    for source in range(strips):
        pltpu.make_async_copy(
            mixed_ref.at[0], out_ref.at[source], recv_sem.at[source]
        ).wait()


def scan_call(first, slabs, gates, decay_rate, beta_bias, per_group, tall, wide, dk):
    strips, block, width = slabs.shape[1:]
    count = strips * block
    chunk = min(128, count)
    vmem = pl.BlockSpec(memory_space=pltpu.VMEM)
    smem = pl.BlockSpec(memory_space=pltpu.SMEM)
    return pl.pallas_call(
        functools.partial(scan_kernel, (chunk, per_group, tall, wide, dk)),
        out_shape=jax.ShapeDtypeStruct((strips, block, width), bf16),
        in_specs=[smem, vmem, vmem, smem, smem],
        out_specs=vmem,
        scratch_shapes=[
            pltpu.VMEM((3, count, width), f32),
            pltpu.VMEM((2 * per_group, count, chunk), f32),
            pltpu.VMEM((count, width), f32),
            pltpu.VMEM((count, width), f32),
            pltpu.VMEM((2, width, width), f32),
        ],
        name="scans",
    )(first, slabs, gates, decay_rate, beta_bias)


def on_device(faces, strips, pixels_in, w_qkv, w_gate, decay_rate, beta_bias):
    _, rows_here, wide, features = pixels_in.shape
    heads = decay_rate.shape[0]
    block = rows_here * wide
    tall = rows_here * strips
    model = w_qkv.shape[1] * faces // 3
    dk = model // heads
    groups = min(strips, heads)
    rep = strips // groups
    per_group = heads // groups
    width = per_group * dk
    n_slab = w_qkv.shape[1] // width
    gate_cols = w_gate.shape[1]
    n_gate = gate_cols // per_group
    vmem = pl.BlockSpec(memory_space=pltpu.VMEM)
    dma = pltpu.SemaphoreType.DMA
    slabs, gates = pl.pallas_call(
        functools.partial(project_kernel, (faces, strips, groups, rep, heads, per_group)),
        out_shape=(
            jax.ShapeDtypeStruct((3, strips, block, width), bf16),
            jax.ShapeDtypeStruct((2, strips, gate_cols, block), f32),
        ),
        in_specs=[vmem, vmem, vmem],
        out_specs=(vmem, vmem),
        scratch_shapes=[
            pltpu.VMEM((faces, block, features), bf16),
            pltpu.VMEM((faces, n_slab, block, width), bf16),
            pltpu.VMEM((faces, gate_cols, block), f32),
            dma((faces,)),
            dma((faces,)),
            dma((faces, n_slab, rep)),
            dma((3, strips)),
            dma((faces, n_gate, rep)),
            dma((2, strips)),
        ],
        compiler_params=pltpu.CompilerParams(collective_id=0, has_side_effects=True),
        name="project",
    )(pixels_in.reshape(block, features), w_qkv, w_gate)
    first = (lax.axis_index("strip") // rep * per_group).astype(jnp.int32).reshape(1)
    mixed = scan_call(first, slabs, gates, decay_rate, beta_bias, per_group, tall, wide, dk)
    returned = pl.pallas_call(
        functools.partial(return_kernel, faces, strips),
        out_shape=jax.ShapeDtypeStruct((strips, block, width), bf16),
        in_specs=[vmem],
        out_specs=vmem,
        scratch_shapes=[dma((strips,)), dma((strips,))],
        compiler_params=pltpu.CompilerParams(collective_id=1, has_side_effects=True),
        name="give_back",
    )(mixed)
    whole = returned[::rep].transpose(1, 0, 2)
    return whole.reshape(1, rows_here, wide, model)


def solution(mesh):
    in_specs = (P("face", "strip", None, None), P(None, "face"), P(None, "face"), P(), P())
    out_specs = P("face", "strip", None, None)
    return jax.shard_map(
        functools.partial(on_device, mesh.shape["face"], mesh.shape["strip"]),
        mesh=mesh,
        in_specs=in_specs,
        out_specs=out_specs,
        check_vma=False,
    )
```

```python
import functools

import jax
import jax.numpy as jnp
from jax import lax
from jax.experimental import pallas as pl
from jax.experimental.pallas import tpu as pltpu
from jax.sharding import PartitionSpec as P

MESH = pl.DeviceIdType.MESH
f32 = jnp.float32
bf16 = jnp.bfloat16


def group_of(place, strips, groups):
    rep = strips // groups
    if rep > 1 or groups % 2:
        return place // rep
    return jnp.where(lax.rem(place, 2) == 0, place // 2, groups - 1 - place // 2)


def project_kernel(
    cfg, px_ref, wq_ref, wg_ref, slabs_ref, gates_ref,
    px_all, wbuf, wg_own, wg_all, acc, px_send, px_fwd, px_recv, w_send, w_recv, g_send, g_recv,
):
    faces, strips, groups, n_slab, pieces = cfg
    me_f, me_s = lax.axis_index("face"), lax.axis_index("strip")
    block, features = px_ref.shape
    count = strips * block
    width = wbuf.shape[2]
    chips = strips // 2
    core, chip = lax.rem(me_s, 2), me_s // 2
    partner = chip * 2 + (1 - core)
    group = group_of(me_s, strips, groups)
    depth = features // pieces

    def chip_at(step):
        return lax.rem(chip + step, chips) * 2 + core

    barrier = pltpu.get_barrier_semaphore()

    def greet(face, strip):
        pl.semaphore_signal(barrier, inc=1, device_id=(face, strip), device_id_type=MESH)

    greet(me_f, partner)
    for step in range(1, chips):
        greet(me_f, chip_at(step))
    for step in range(1, faces):
        greet(lax.rem(me_f + step, faces), me_s)

    wg_own[...] = wg_ref[...].astype(f32)

    def rows_of(strip):
        return px_all.at[pl.ds(pl.multiple_of(strip * block, block), block)]

    own_px = pltpu.make_async_copy(px_ref, rows_of(me_s), px_recv.at[me_s])
    own_px.start()
    pl.semaphore_wait(barrier, 1 + chips - 1 + faces - 1)

    def weight_from(kind):
        slab = kind * groups + group
        return slab // n_slab, lax.rem(slab, n_slab)

    def weight_src(j, p):
        rows = pl.ds(p * depth, depth)
        if len(wq_ref.shape) == 3:
            return wq_ref.at[j, rows]
        return wq_ref.at[rows, pl.ds(pl.multiple_of(j * width, width), width)]

    def weight_copy(kind, p, src, side):
        return pltpu.make_async_remote_copy(
            src_ref=src,
            dst_ref=wbuf.at[kind, pl.ds(p * depth, depth)],
            send_sem=w_send.at[kind, p, side],
            recv_sem=w_recv.at[kind, p],
            device_id=(me_f + (1 if side else -1), me_s),
            device_id_type=MESH,
        )

    def own_weight(kind, p, j):
        return pltpu.make_async_copy(
            weight_src(j, p), wbuf.at[kind, pl.ds(p * depth, depth)], w_recv.at[kind, p]
        )

    for p in range(pieces):
        for kind in range(3):
            owner, j = weight_from(kind)

            @pl.when(owner == me_f)
            def _(kind=kind, p=p, j=j):
                pl.when(me_f + 1 < faces)(weight_copy(kind, p, weight_src(j, p), 1).start)
                pl.when(me_f > 0)(weight_copy(kind, p, weight_src(j, p), 0).start)
                own_weight(kind, p, j).start()

    def px_copy(dest, sem, source, src):
        return pltpu.make_async_remote_copy(
            src_ref=src,
            dst_ref=rows_of(source),
            send_sem=sem,
            recv_sem=px_recv.at[source],
            device_id=(me_f, dest),
            device_id_type=MESH,
        )

    def px_out(step):
        return px_copy(chip_at(step), px_send.at[step], me_s, px_ref)

    def px_pass(step):
        source = chip_at(step)
        return px_copy(partner, px_fwd.at[step], source, rows_of(source))

    to_partner = px_copy(partner, px_send.at[0], me_s, px_ref)
    for step in range(1, chips):
        px_out(step).start()
    to_partner.start()

    def gate_copy(step):
        return pltpu.make_async_remote_copy(
            src_ref=wg_own,
            dst_ref=wg_all.at[me_f],
            send_sem=g_send.at[step],
            recv_sem=g_recv.at[me_f],
            device_id=(lax.rem(me_f + step, faces), me_s),
            device_id_type=MESH,
        )

    for step in range(1, faces):
        gate_copy(step).start()
    own_gate = pltpu.make_async_copy(wg_own, wg_all.at[me_f], g_recv.at[me_f])
    own_gate.start()

    def px_wait(strip):
        pltpu.make_async_copy(px_ref, rows_of(strip), px_recv.at[strip]).wait()

    def pass_pixels(step):
        px_wait(chip_at(step))
        px_pass(step).start()

    def pass_weights(p):
        for kind in range(3):
            owner, _ = weight_from(kind)
            here = wbuf.at[kind, pl.ds(p * depth, depth)]
            pltpu.make_async_copy(here, here, w_recv.at[kind, p]).wait()
            pl.when((owner < me_f) & (me_f + 1 < faces))(weight_copy(kind, p, here, 1).start)
            pl.when((owner > me_f) & (me_f > 0))(weight_copy(kind, p, here, 0).start)

    tile = min(512, count)

    def each_tile(body):
        if count == tile:
            body(pl.ds(0, tile), 0)
        else:

            def one(i, carry):
                body(pl.ds(pl.multiple_of(i * tile, tile), tile), i)
                return carry

            lax.fori_loop(0, count // tile, one, 0)

    def multiply(p):
        rows = pl.ds(p * depth, depth)
        weights = jnp.concatenate([wbuf[kind, rows, :] for kind in range(3)], axis=1)

        def body(at, _):
            term = jnp.dot(px_all[at, rows], weights, preferred_element_type=f32)
            if p > 0:
                term = term + acc[at, :]
            if p < pieces - 1:
                acc[at, :] = term
            else:
                for kind in range(3):
                    slabs_ref[kind, at, :] = term[
                        :, kind * width : (kind + 1) * width
                    ].astype(bf16)

        each_tile(body)

    for turn in range(max(pieces - 1, chips - 1)):
        if turn < pieces - 1:
            pass_weights(turn)
        if turn < chips - 1:
            pass_pixels(turn + 1)
    px_wait(me_s)
    px_wait(partner)
    for step in range(1, chips):
        px_wait(lax.rem(chip + step, chips) * 2 + (1 - core))
    for face in range(faces):
        pltpu.make_async_copy(wg_own, wg_all.at[face], g_recv.at[face]).wait()
    gate_w = jnp.concatenate([wg_all[face] for face in range(faces)], axis=0).astype(bf16)

    chunk = gates_ref.shape[2]

    def gate_body(at, i):
        logits = lax.dot_general(
            gate_w, px_all[at, :], (((1,), (1,)), ((), ())), preferred_element_type=f32
        )
        logits = logits.astype(bf16).astype(f32)
        for c in range(tile // chunk):
            gates_ref[i * (tile // chunk) + c] = logits[:, c * chunk : (c + 1) * chunk]

    each_tile(gate_body)
    for p in range(pieces - 1):
        multiply(p)
    pass_weights(pieces - 1)
    multiply(pieces - 1)

    to_partner.wait_send()
    for step in range(1, chips):
        px_out(step).wait_send()
        px_pass(step).wait_send()
    for step in range(1, faces):
        gate_copy(step).wait_send()
    for p in range(pieces):
        for kind in range(3):
            owner, _ = weight_from(kind)
            here = wbuf.at[kind, pl.ds(p * depth, depth)]
            pl.when((owner <= me_f) & (me_f + 1 < faces))(
                weight_copy(kind, p, here, 1).wait_send
            )
            pl.when((owner >= me_f) & (me_f > 0))(weight_copy(kind, p, here, 0).wait_send)


def mm(a, b, dims=((1,), (0,))):
    return lax.dot_general(
        a.astype(bf16), b.astype(bf16), (dims, ((), ())), preferred_element_type=f32
    )


def split_mm(exact, wide, pieces):
    exact = exact.astype(bf16)
    total, rest = None, wide
    for _ in range(pieces):
        piece = rest.astype(bf16)
        rest = rest - piece.astype(f32)
        term = jnp.dot(exact, piece, preferred_element_type=f32)
        total = term if total is None else total + term
    return total


def mm_split(wide, exact, pieces):
    exact = exact.astype(bf16)
    total, rest = None, wide
    for _ in range(pieces):
        piece = rest.astype(bf16)
        rest = rest - piece.astype(f32)
        term = jnp.dot(piece, exact, preferred_element_type=f32)
        total = term if total is None else total + term
    return total


def scan_kernel(
    cfg, first_ref, slabs_ref, gates_ref, rate_ref, bias_ref, out_ref,
    feats, gates, row_buf, col_buf, states,
):
    chunk, per_group, tall, wide, dk = cfg
    count, width = slabs_ref.shape[1:]
    strips, block, _ = out_ref.shape
    heads = gates_ref.shape[1] // 2
    first = first_ref[0]

    lane = lax.broadcasted_iota(jnp.int32, (width, width), 1)
    sub = lax.broadcasted_iota(jnp.int32, (width, width), 0)
    same_head = (lane // dk) == (sub // dk)
    head_ones = same_head.astype(f32)
    ti = lax.broadcasted_iota(jnp.int32, (chunk, chunk), 0)
    tj = lax.broadcasted_iota(jnp.int32, (chunk, chunk), 1)
    inclusive = ti >= tj
    tri = inclusive.astype(f32)
    eye = (ti == tj).astype(f32)

    def prepare(i, carry):
        at = pl.ds(pl.multiple_of(i * chunk, chunk), chunk)
        for kind in range(3):
            x = slabs_ref[kind, at, :].astype(f32)
            if kind < 2:
                x = x * lax.rsqrt(mm_split(x * x, head_ones, 2) + 1e-06)
            feats[kind, at, :] = x
        for a in range(per_group):
            head = first + a
            decay = -rate_ref[head] * jnp.exp(gates_ref[i, pl.ds(head, 1), :])
            strength = jax.nn.sigmoid(gates_ref[i, pl.ds(heads + head, 1), :] + bias_ref[head])
            gates[a, at, :] = jnp.broadcast_to(decay, (chunk, chunk)).T
            gates[per_group + a, at, :] = jnp.broadcast_to(strength, (chunk, chunk)).T
        return carry

    lax.fori_loop(0, count // chunk, prepare, 0, unroll=count // chunk <= 4)

    columns = chunk // tall
    flane = lax.broadcasted_iota(jnp.int32, (chunk, width), 1) // dk

    def lanes_of(parts):
        out = parts[0][:, :width]
        for a in range(1, per_group):
            out = jnp.where(flane == a, parts[a][:, :width], out)
        return out

    def stacked(x):
        if per_group == 1:
            return x
        return jnp.concatenate(
            [jnp.where(flane == a, x, jnp.zeros_like(x)) for a in range(per_group)], axis=0
        )

    def side_by_side(parts):
        return parts[0] if per_group == 1 else jnp.concatenate(parts, axis=1)

    def load(ref, which, i, by_column):
        if not by_column:
            return ref[which, pl.ds(pl.multiple_of(i * chunk, chunk), chunk), :]
        return jnp.concatenate(
            [ref[which, pl.ds(i * columns + c, tall, stride=wide), :] for c in range(columns)],
            axis=0,
        )

    states[...] = jnp.zeros_like(states)

    def advance(i, carry):
        work = []
        for order in range(2):
            q, k, v = (load(feats, kind, i, order) for kind in range(3))
            cums, betas, systems, scores = [], [], [], []
            for a in range(per_group):
                cum = split_mm(tri, load(gates, a, i, order), 3)
                beta = load(gates, per_group + a, i, order)
                gap = cum - cum.T
                within = jnp.where(inclusive, jnp.exp(jnp.where(inclusive, gap, 0.0)), 0.0)
                k_a = k if per_group == 1 else jnp.where(flane == a, k, 0.0)
                q_a = q if per_group == 1 else jnp.where(flane == a, q, 0.0)
                dots = mm(jnp.concatenate([k_a, q_a], axis=0), k, ((1,), (1,)))
                systems.append(within * dots[:chunk] * beta)
                scores.append(within * dots[chunk:])
                cums.append(cum)
                betas.append(beta)
            work.append((q, k, v, cums, betas, systems, scores))

        inverses = [[None] * per_group for _ in range(2)]
        half = 1
        while half < chunk:
            here = ((ti // (2 * half)) == (tj // (2 * half))) & (
                (lax.rem(ti, 2 * half) >= half) & (lax.rem(tj, 2 * half) < half)
            )
            lows = [
                [jnp.where(here, work[o][5][a], 0.0) for a in range(per_group)] for o in range(2)
            ]
            if half == 1:
                inverses = [[eye - low for low in row] for row in lows]
            else:
                firsts = [
                    [mm(lows[o][a], inverses[o][a]) for a in range(per_group)] for o in range(2)
                ]
                inverses = [
                    [inverses[o][a] - mm(inverses[o][a], firsts[o][a]) for a in range(per_group)]
                    for o in range(2)
                ]
            half *= 2

        for order in range(2):
            q, k, v, cums, betas, _, scores = work[order]
            beta = lanes_of(betas)
            cum = lanes_of(cums)
            scale = jnp.exp(cum)
            last = cum[chunk - 1 : chunk, :]
            tail = jnp.exp(last - cum)
            both = side_by_side(inverses[order])
            u = mm(both, stacked(v * beta))
            w = mm(both, stacked(k * (beta * scale)))
            state = states[order]
            fresh = u - mm(w, state)
            out = mm(q * scale, state) + mm(side_by_side(scores), stacked(fresh))
            grown = mm(k * tail, fresh, ((0,), (0,)))
            decayed = state * jnp.exp(last)
            states[order] = decayed + jnp.where(same_head, grown, 0.0)
            normed = out * lax.rsqrt(mm_split(out * out, head_ones, 2) * (1.0 / dk) + 1e-06)
            if order == 0:
                row_buf[pl.ds(pl.multiple_of(i * chunk, chunk), chunk), :] = normed
            else:
                normed = normed.astype(bf16).astype(f32)
                for c in range(columns):
                    col_buf[pl.ds(i * columns + c, tall, stride=wide), :] = normed[
                        c * tall : (c + 1) * tall
                    ]
        return carry

    lax.fori_loop(0, count // chunk, advance, 0)

    def finish(s, carry):
        at = pl.ds(s * block, block)
        out_ref[s] = (row_buf[at, :] + col_buf[at, :]).astype(bf16)
        return carry

    lax.fori_loop(0, strips, finish, 0)


def return_kernel(strips, groups, mixed_ref, out_ref, send_sem, recv_sem):
    me_f, me_s = lax.axis_index("face"), lax.axis_index("strip")
    rep = strips // groups
    barrier = pltpu.get_barrier_semaphore()
    for step in range(1, strips):
        pl.semaphore_signal(
            barrier, inc=1, device_id=(me_f, lax.rem(me_s + step, strips)), device_id_type=MESH
        )
    pl.semaphore_wait(barrier, strips - 1)
    mine = group_of(me_s, strips, groups)
    sends = lax.rem(me_s, rep) == 0

    def copy(step):
        dest = lax.rem(me_s + step, strips)
        return pltpu.make_async_remote_copy(
            src_ref=mixed_ref.at[dest],
            dst_ref=out_ref.at[mine],
            send_sem=send_sem.at[step],
            recv_sem=recv_sem.at[mine],
            device_id=(me_f, dest),
            device_id_type=MESH,
        )

    @pl.when(sends)
    def _():
        for step in range(1, strips):
            copy(step).start()
        pltpu.make_async_copy(mixed_ref.at[me_s], out_ref.at[mine], recv_sem.at[mine]).start()
        for step in range(1, strips):
            copy(step).wait_send()

    for group in range(groups):
        pltpu.make_async_copy(mixed_ref.at[0], out_ref.at[group], recv_sem.at[group]).wait()


def scan_call(
    first, slabs, gates, decay_rate, beta_bias, strips, per_group, tall, wide, dk
):
    count, width = slabs.shape[1:]
    block = count // strips
    chunk = min(128, count)
    vmem = pl.BlockSpec(memory_space=pltpu.VMEM)
    smem = pl.BlockSpec(memory_space=pltpu.SMEM)
    return pl.pallas_call(
        functools.partial(scan_kernel, (chunk, per_group, tall, wide, dk)),
        out_shape=jax.ShapeDtypeStruct((strips, block, width), bf16),
        in_specs=[smem, vmem, vmem, smem, smem],
        out_specs=vmem,
        scratch_shapes=[
            pltpu.VMEM((3, count, width), f32),
            pltpu.VMEM((2 * per_group, count, chunk), f32),
            pltpu.VMEM((count, width), f32),
            pltpu.VMEM((count, width), f32),
            pltpu.VMEM((2, width, width), f32),
        ],
        name="scans",
    )(first, slabs, gates, decay_rate, beta_bias)


def on_device(faces, strips, pixels_in, w_qkv, w_gate, decay_rate, beta_bias):
    _, rows_here, wide, features = pixels_in.shape
    heads = decay_rate.shape[0]
    block = rows_here * wide
    count = block * strips
    tall = rows_here * strips
    model = w_qkv.shape[1] * faces // 3
    dk = model // heads
    groups = min(strips, heads)
    per_group = heads // groups
    width = per_group * dk
    n_slab = w_qkv.shape[1] // width
    gate_cols = w_gate.shape[1]
    pieces = 4
    chunk = min(128, count)
    chips = strips // 2
    vmem = pl.BlockSpec(memory_space=pltpu.VMEM)
    dma = pltpu.SemaphoreType.DMA
    if width % 128:
        w_qkv = w_qkv.reshape(features, n_slab, width).transpose(1, 0, 2)
    slabs, gates = pl.pallas_call(
        functools.partial(project_kernel, (faces, strips, groups, n_slab, pieces)),
        out_shape=(
            jax.ShapeDtypeStruct((3, count, width), bf16),
            jax.ShapeDtypeStruct((count // chunk, 2 * heads, chunk), f32),
        ),
        in_specs=[vmem, pl.BlockSpec(memory_space=pl.ANY), vmem],
        out_specs=(vmem, vmem),
        scratch_shapes=[
            pltpu.VMEM((count, features), bf16),
            pltpu.VMEM((3, features, width), bf16),
            pltpu.VMEM((gate_cols, features), f32),
            pltpu.VMEM((faces, gate_cols, features), f32),
            pltpu.VMEM((count, 3 * width), f32),
            dma((chips,)),
            dma((chips,)),
            dma((strips,)),
            dma((3, pieces, 2)),
            dma((3, pieces)),
            dma((faces,)),
            dma((faces,)),
        ],
        compiler_params=pltpu.CompilerParams(collective_id=0, has_side_effects=True),
        name="project",
    )(pixels_in.reshape(block, features), w_qkv, w_gate.T)
    group = group_of(lax.axis_index("strip"), strips, groups)
    first = (group * per_group).astype(jnp.int32).reshape(1)
    mixed = scan_call(
        first, slabs, gates, decay_rate, beta_bias, strips, per_group, tall, wide, dk
    )
    returned = pl.pallas_call(
        functools.partial(return_kernel, strips, groups),
        out_shape=jax.ShapeDtypeStruct((groups, block, width), bf16),
        in_specs=[vmem],
        out_specs=vmem,
        scratch_shapes=[dma((strips,)), dma((groups,))],
        compiler_params=pltpu.CompilerParams(collective_id=1, has_side_effects=True),
        name="give_back",
    )(mixed)
    return returned.transpose(1, 0, 2).reshape(1, rows_here, wide, model)


def solution(mesh):
    in_specs = (P("face", "strip", None, None), P(None, "face"), P(None, "face"), P(), P())
    out_specs = P("face", "strip", None, None)
    return jax.shard_map(
        functools.partial(on_device, mesh.shape["face"], mesh.shape["strip"]),
        mesh=mesh,
        in_specs=in_specs,
        out_specs=out_specs,
        check_vma=False,
    )
```

```python
import functools

import jax
import jax.numpy as jnp
from jax import lax
from jax.experimental import pallas as pl
from jax.experimental.pallas import tpu as pltpu
from jax.sharding import PartitionSpec as P

MESH = pl.DeviceIdType.MESH
f32 = jnp.float32
bf16 = jnp.bfloat16


def greet_all(faces, strips, me_f, me_s):
    barrier = pltpu.get_barrier_semaphore()
    total = faces * strips
    me = me_f * strips + me_s

    def one(step, carry):
        other = lax.rem(me + step, total)
        pl.semaphore_signal(
            barrier,
            inc=1,
            device_id=(other // strips, lax.rem(other, strips)),
            device_id_type=MESH,
        )
        return carry

    lax.fori_loop(1, total, one, 0)
    pl.semaphore_wait(barrier, total - 1)


def project_kernel(
    cfg, px_ref, wq_ref, wg_ref, slabs_ref, gates_ref,
    px_all, proj, glog, weights, weight_sem, px_send, px_recv, slab_send, slab_recv, gate_send, gate_recv,
):
    faces, strips, groups, rep, heads, per_group = cfg
    me_f, me_s = lax.axis_index("face"), lax.axis_index("strip")
    n_slab = proj.shape[1]
    gate_cols = wg_ref.shape[0]
    width = proj.shape[3]
    n_gate = gate_cols // per_group
    block = px_ref.shape[0]
    half = block // 2
    fetch = pltpu.make_async_copy(wq_ref, weights, weight_sem)
    fetch.start()
    greet_all(faces, strips, me_f, me_s)
    two_sided = jnp.minimum(me_f, faces - 1 - me_f)
    longer = jnp.where(me_f < faces - 1 - me_f, 1, -1)

    def face_at(step):
        near = me_f + (step + 1) // 2 * (-1 if step % 2 else 1)
        return jnp.where(step <= 2 * two_sided, near, me_f + longer * (step - two_sided))

    def px_copy(face, dest, piece, sem, src):
        rows = pl.ds(piece * half, half)
        return pltpu.make_async_remote_copy(
            src_ref=src.at[rows],
            dst_ref=px_all.at[face, rows],
            send_sem=sem,
            recv_sem=px_recv.at[face, piece],
            device_id=(dest, me_s),
            device_id_type=MESH,
        )

    def px_out(piece, side):
        dest = me_f + (1 if side else -1)
        there = (dest >= 0) & (dest < faces)
        return there, px_copy(me_f, dest, piece, px_send.at[0, piece, side], px_ref)

    def px_pass(step, piece):
        face = face_at(step)
        dest = jnp.where(face < me_f, me_f + 1, me_f - 1)
        there = (dest >= 0) & (dest < faces)
        return there, px_copy(face, dest, piece, px_send.at[step, piece, 0], px_all.at[face])

    for piece in range(2):
        for side in range(2):
            there, copy = px_out(piece, side)
            pl.when(there)(copy.start)

    def slab_copy(step, j, r):
        face = face_at(step) if step else me_f
        slab = me_f * n_slab + j
        kind, group = slab // groups, lax.rem(slab, groups)
        dest = group * rep + r
        remote = pltpu.make_async_remote_copy(
            src_ref=proj.at[step, j],
            dst_ref=slabs_ref.at[kind, me_s],
            send_sem=slab_send.at[step, j, r],
            recv_sem=slab_recv.at[kind, me_s],
            device_id=(face, dest),
            device_id_type=MESH,
        )
        local = pltpu.make_async_copy(
            proj.at[step, j], slabs_ref.at[kind, me_s], slab_recv.at[kind, me_s]
        )
        return remote, local, dest

    def gate_copy(step, i, r):
        face = face_at(step) if step else me_f
        first = me_f * gate_cols
        kind, group = first // heads, lax.rem(first, heads) // per_group + i
        dest = group * rep + r
        remote = pltpu.make_async_remote_copy(
            src_ref=glog.at[step],
            dst_ref=gates_ref.at[kind, me_s],
            send_sem=gate_send.at[step, i, r],
            recv_sem=gate_recv.at[kind, me_s],
            device_id=(face, dest),
            device_id_type=MESH,
        )
        local = pltpu.make_async_copy(
            glog.at[step], gates_ref.at[kind, me_s], gate_recv.at[kind, me_s]
        )
        return remote, local, dest

    def launch(copies, step):
        remote, local, dest = copies
        if step == 0:
            pl.when(dest == me_s)(local.start)
            pl.when(dest != me_s)(remote.start)
        else:
            remote.start()

    def drain(copies, step):
        remote, _, dest = copies
        if step == 0:
            pl.when(dest != me_s)(remote.wait_send)
        else:
            remote.wait_send()

    for step in range(faces):
        if step == 0:
            px = px_ref[...]
        else:
            face = face_at(step) if step else me_f
            for piece in range(2):
                rows = pl.ds(piece * half, half)
                pltpu.make_async_copy(
                    px_ref.at[rows], px_all.at[face, rows], px_recv.at[face, piece]
                ).wait()
                there, copy = px_pass(step, piece)
                pl.when(there)(copy.start)
            px = px_all[face]
        logits = lax.dot_general(
            wg_ref[...], px, (((1,), (1,)), ((), ())), preferred_element_type=f32
        )
        glog[step] = logits.astype(bf16).astype(f32)
        for i in range(n_gate):
            for r in range(rep):
                launch(gate_copy(step, i, r), step)
        if step == 0:
            fetch.wait()
        whole = jnp.dot(px, weights[...], preferred_element_type=f32).astype(bf16)
        for j in range(n_slab):
            proj[step, j] = whole[:, j * width : (j + 1) * width]
        for j in range(n_slab):
            for r in range(rep):
                launch(slab_copy(step, j, r), step)

    for piece in range(2):
        for side in range(2):
            there, copy = px_out(piece, side)
            pl.when(there)(copy.wait_send)
        for step in range(1, faces):
            there, copy = px_pass(step, piece)
            pl.when(there)(copy.wait_send)
    for step in range(faces):
        for i in range(n_gate):
            for r in range(rep):
                drain(gate_copy(step, i, r), step)
        for j in range(n_slab):
            for r in range(rep):
                drain(slab_copy(step, j, r), step)
    for source in range(strips):
        for kind in range(slabs_ref.shape[0]):
            pltpu.make_async_copy(
                proj.at[0, 0], slabs_ref.at[kind, source], slab_recv.at[kind, source]
            ).wait()
        for kind in range(gates_ref.shape[0]):
            pltpu.make_async_copy(
                glog.at[0], gates_ref.at[kind, source], gate_recv.at[kind, source]
            ).wait()


def mm(a, b, dims=((1,), (0,))):
    return lax.dot_general(
        a.astype(bf16), b.astype(bf16), (dims, ((), ())), preferred_element_type=f32
    )


def split_mm(exact, wide, pieces):
    exact = exact.astype(bf16)
    total, rest = None, wide
    for _ in range(pieces):
        piece = rest.astype(bf16)
        rest = rest - piece.astype(f32)
        term = jnp.dot(exact, piece, preferred_element_type=f32)
        total = term if total is None else total + term
    return total


def mm_split(wide, exact, pieces):
    exact = exact.astype(bf16)
    total, rest = None, wide
    for _ in range(pieces):
        piece = rest.astype(bf16)
        rest = rest - piece.astype(f32)
        term = jnp.dot(piece, exact, preferred_element_type=f32)
        total = term if total is None else total + term
    return total


def scan_kernel(
    cfg, first_ref, slabs_ref, gates_ref, rate_ref, bias_ref, out_ref,
    feats, gates, row_buf, col_buf, states,
):
    chunk, per_group, tall, wide, dk = cfg
    strips, block, width = slabs_ref.shape[1:]
    count = strips * block
    first = first_ref[0]
    gate_cols = gates_ref.shape[2]

    lane = lax.broadcasted_iota(jnp.int32, (width, width), 1)
    sub = lax.broadcasted_iota(jnp.int32, (width, width), 0)
    same_head = (lane // dk) == (sub // dk)
    head_ones = same_head.astype(f32)
    ti = lax.broadcasted_iota(jnp.int32, (chunk, chunk), 0)
    tj = lax.broadcasted_iota(jnp.int32, (chunk, chunk), 1)
    inclusive = ti >= tj
    tri = inclusive.astype(f32)
    eye = (ti == tj).astype(f32)

    def prepare(s, carry):
        at = pl.ds(s * block, block)
        for kind in range(3):
            x = slabs_ref[kind, s].astype(f32)
            if kind < 2:
                x = x * lax.rsqrt(mm_split(x * x, head_ones, 2) + 1e-06)
            feats[kind, at, :] = x
        for a in range(per_group):
            head = first + a
            row = lax.rem(head, gate_cols)
            decay = -rate_ref[head] * jnp.exp(gates_ref[0, s, pl.ds(row, 1), :])
            strength = jax.nn.sigmoid(gates_ref[1, s, pl.ds(row, 1), :] + bias_ref[head])
            gates[a, at, :] = jnp.broadcast_to(decay, (chunk, block)).T
            gates[per_group + a, at, :] = jnp.broadcast_to(strength, (chunk, block)).T
        return carry

    lax.fori_loop(0, strips, prepare, 0, unroll=True if strips <= 8 else 1)

    columns = chunk // tall
    flane = lax.broadcasted_iota(jnp.int32, (chunk, width), 1) // dk

    def lanes_of(parts):
        out = parts[0][:, :width]
        for a in range(1, per_group):
            out = jnp.where(flane == a, parts[a][:, :width], out)
        return out

    def stacked(x):
        if per_group == 1:
            return x
        return jnp.concatenate(
            [jnp.where(flane == a, x, jnp.zeros_like(x)) for a in range(per_group)], axis=0
        )

    def side_by_side(parts):
        return parts[0] if per_group == 1 else jnp.concatenate(parts, axis=1)

    def load(ref, which, i, by_column):
        if not by_column:
            return ref[which, pl.ds(pl.multiple_of(i * chunk, chunk), chunk), :]
        return jnp.concatenate(
            [ref[which, pl.ds(i * columns + c, tall, stride=wide), :] for c in range(columns)],
            axis=0,
        )

    states[...] = jnp.zeros_like(states)

    def advance(i, carry):
        work = []
        for order in range(2):
            q, k, v = (load(feats, kind, i, order) for kind in range(3))
            cums, betas, systems, scores = [], [], [], []
            for a in range(per_group):
                cum = split_mm(tri, load(gates, a, i, order), 3)
                beta = load(gates, per_group + a, i, order)
                gap = cum - cum.T
                within = jnp.where(inclusive, jnp.exp(jnp.where(inclusive, gap, 0.0)), 0.0)
                k_a = k if per_group == 1 else jnp.where(flane == a, k, 0.0)
                q_a = q if per_group == 1 else jnp.where(flane == a, q, 0.0)
                dots = mm(jnp.concatenate([k_a, q_a], axis=0), k, ((1,), (1,)))
                systems.append(within * dots[:chunk] * beta)
                scores.append(within * dots[chunk:])
                cums.append(cum)
                betas.append(beta)
            work.append((q, k, v, cums, betas, systems, scores))

        inverses = [[None] * per_group for _ in range(2)]
        half = 1
        while half < chunk:
            here = ((ti // (2 * half)) == (tj // (2 * half))) & (
                (lax.rem(ti, 2 * half) >= half) & (lax.rem(tj, 2 * half) < half)
            )
            lows = [
                [jnp.where(here, work[o][5][a], 0.0) for a in range(per_group)] for o in range(2)
            ]
            if half == 1:
                inverses = [[eye - low for low in row] for row in lows]
            else:
                firsts = [
                    [mm(lows[o][a], inverses[o][a]) for a in range(per_group)] for o in range(2)
                ]
                inverses = [
                    [inverses[o][a] - mm(inverses[o][a], firsts[o][a]) for a in range(per_group)]
                    for o in range(2)
                ]
            half *= 2

        for order in range(2):
            q, k, v, cums, betas, _, scores = work[order]
            beta = lanes_of(betas)
            cum = lanes_of(cums)
            scale = jnp.exp(cum)
            last = cum[chunk - 1 : chunk, :]
            tail = jnp.exp(last - cum)
            both = side_by_side(inverses[order])
            u = mm(both, stacked(v * beta))
            w = mm(both, stacked(k * (beta * scale)))
            state = states[order]
            fresh = u - mm(w, state)
            out = mm(q * scale, state) + mm(side_by_side(scores), stacked(fresh))
            grown = mm(k * tail, fresh, ((0,), (0,)))
            decayed = state * jnp.exp(last)
            states[order] = decayed + jnp.where(same_head, grown, 0.0)
            normed = out * lax.rsqrt(mm_split(out * out, head_ones, 2) * (1.0 / dk) + 1e-06)
            if order == 0:
                row_buf[pl.ds(pl.multiple_of(i * chunk, chunk), chunk), :] = normed
            else:
                normed = normed.astype(bf16).astype(f32)
                for c in range(columns):
                    col_buf[pl.ds(i * columns + c, tall, stride=wide), :] = normed[
                        c * tall : (c + 1) * tall
                    ]
        return carry

    lax.fori_loop(0, count // chunk, advance, 0)

    def finish(s, carry):
        at = pl.ds(s * block, block)
        out_ref[s] = (row_buf[at, :] + col_buf[at, :]).astype(bf16)
        return carry

    lax.fori_loop(0, strips, finish, 0)


def return_kernel(rep, strips, mixed_ref, out_ref, send_sem, recv_sem):
    me_f, me_s = lax.axis_index("face"), lax.axis_index("strip")
    barrier = pltpu.get_barrier_semaphore()
    for step in range(1, strips):
        pl.semaphore_signal(
            barrier, inc=1, device_id=(me_f, lax.rem(me_s + step, strips)), device_id_type=MESH
        )
    pl.semaphore_wait(barrier, strips - 1)

    width = mixed_ref.shape[2]
    mine = me_s // rep

    def place(group):
        if len(out_ref.shape) == 3:
            return out_ref.at[group]
        return out_ref.at[:, pl.ds(pl.multiple_of(group * width, width), width)]

    def copy(step):
        dest = lax.rem(me_s + step, strips)
        return pltpu.make_async_remote_copy(
            src_ref=mixed_ref.at[dest],
            dst_ref=place(mine),
            send_sem=send_sem.at[step],
            recv_sem=recv_sem.at[mine],
            device_id=(me_f, dest),
            device_id_type=MESH,
        )

    @pl.when(lax.rem(me_s, rep) == 0)
    def _():
        for step in range(1, strips):
            copy(step).start()
        pltpu.make_async_copy(mixed_ref.at[me_s], place(mine), recv_sem.at[mine]).start()
        for step in range(1, strips):
            copy(step).wait_send()

    for group in range(strips // rep):
        pltpu.make_async_copy(mixed_ref.at[0], place(group), recv_sem.at[group]).wait()


def scan_call(first, slabs, gates, decay_rate, beta_bias, per_group, tall, wide, dk):
    strips, block, width = slabs.shape[1:]
    count = strips * block
    chunk = min(128, count)
    vmem = pl.BlockSpec(memory_space=pltpu.VMEM)
    smem = pl.BlockSpec(memory_space=pltpu.SMEM)
    return pl.pallas_call(
        functools.partial(scan_kernel, (chunk, per_group, tall, wide, dk)),
        out_shape=jax.ShapeDtypeStruct((strips, block, width), bf16),
        in_specs=[smem, vmem, vmem, smem, smem],
        out_specs=vmem,
        scratch_shapes=[
            pltpu.VMEM((3, count, width), f32),
            pltpu.VMEM((2 * per_group, count, chunk), f32),
            pltpu.VMEM((count, width), f32),
            pltpu.VMEM((count, width), f32),
            pltpu.VMEM((2, width, width), f32),
        ],
        name="scans",
    )(first, slabs, gates, decay_rate, beta_bias)


def on_device(faces, strips, pixels_in, w_qkv, w_gate, decay_rate, beta_bias):
    _, rows_here, wide, features = pixels_in.shape
    heads = decay_rate.shape[0]
    block = rows_here * wide
    tall = rows_here * strips
    model = w_qkv.shape[1] * faces // 3
    dk = model // heads
    groups = min(strips, heads)
    rep = strips // groups
    per_group = heads // groups
    width = per_group * dk
    n_slab = w_qkv.shape[1] // width
    gate_cols = w_gate.shape[1]
    n_gate = gate_cols // per_group
    vmem = pl.BlockSpec(memory_space=pltpu.VMEM)
    dma = pltpu.SemaphoreType.DMA
    slabs, gates = pl.pallas_call(
        functools.partial(project_kernel, (faces, strips, groups, rep, heads, per_group)),
        out_shape=(
            jax.ShapeDtypeStruct((3, strips, block, width), bf16),
            jax.ShapeDtypeStruct((2, strips, gate_cols, block), f32),
        ),
        in_specs=[vmem, pl.BlockSpec(memory_space=pl.ANY), vmem],
        out_specs=(vmem, vmem),
        scratch_shapes=[
            pltpu.VMEM((faces, block, features), bf16),
            pltpu.VMEM((faces, n_slab, block, width), bf16),
            pltpu.VMEM((faces, gate_cols, block), f32),
            pltpu.VMEM(w_qkv.shape, bf16),
            dma(()),
            dma((faces, 2, 2)),
            dma((faces, 2)),
            dma((faces, n_slab, rep)),
            dma((3, strips)),
            dma((faces, n_gate, rep)),
            dma((2, strips)),
        ],
        compiler_params=pltpu.CompilerParams(collective_id=0, has_side_effects=True),
        name="project",
    )(pixels_in.reshape(block, features), w_qkv, w_gate.T)
    first = (lax.axis_index("strip") // rep * per_group).astype(jnp.int32).reshape(1)
    mixed = scan_call(first, slabs, gates, decay_rate, beta_bias, per_group, tall, wide, dk)
    flat = width % 128 == 0
    returned = pl.pallas_call(
        functools.partial(return_kernel, rep, strips),
        out_shape=jax.ShapeDtypeStruct(
            (block, model) if flat else (groups, block, width), bf16
        ),
        in_specs=[vmem],
        out_specs=vmem,
        scratch_shapes=[dma((strips,)), dma((groups,))],
        compiler_params=pltpu.CompilerParams(collective_id=1, has_side_effects=True),
        name="give_back",
    )(mixed)
    if not flat:
        returned = returned.transpose(1, 0, 2)
    return returned.reshape(1, rows_here, wide, model)


def solution(mesh):
    in_specs = (P("face", "strip", None, None), P(None, "face"), P(None, "face"), P(), P())
    out_specs = P("face", "strip", None, None)
    return jax.shard_map(
        functools.partial(on_device, mesh.shape["face"], mesh.shape["strip"]),
        mesh=mesh,
        in_specs=in_specs,
        out_specs=out_specs,
        check_vma=False,
    )
```

```python
import functools

import jax
import jax.numpy as jnp
from jax import lax
from jax.experimental import pallas as pl
from jax.experimental.pallas import tpu as pltpu
from jax.sharding import PartitionSpec as P

MESH = pl.DeviceIdType.MESH
f32 = jnp.float32
bf16 = jnp.bfloat16


def greet_all(faces, strips, me_f, me_s):
    barrier = pltpu.get_barrier_semaphore()
    total = faces * strips
    me = me_f * strips + me_s

    def one(step, carry):
        other = lax.rem(me + step, total)
        pl.semaphore_signal(
            barrier,
            inc=1,
            device_id=(other // strips, lax.rem(other, strips)),
            device_id_type=MESH,
        )
        return carry

    lax.fori_loop(1, total, one, 0)
    pl.semaphore_wait(barrier, total - 1)


def project_kernel(
    cfg, px_ref, wq_ref, wg_ref, slabs_ref, gates_ref,
    px_all, proj, glog, weights, weight_sem, px_send, px_recv, slab_send, slab_recv, gate_send, gate_recv,
):
    faces, strips, groups, rep, heads, per_group = cfg
    me_f, me_s = lax.axis_index("face"), lax.axis_index("strip")
    n_slab = proj.shape[1]
    gate_cols = wg_ref.shape[0]
    width = proj.shape[3]
    n_gate = gate_cols // per_group
    block = px_ref.shape[0]
    half = block // 2
    fetch = pltpu.make_async_copy(wq_ref, weights, weight_sem)
    fetch.start()
    greet_all(faces, strips, me_f, me_s)
    two_sided = jnp.minimum(me_f, faces - 1 - me_f)
    longer = jnp.where(me_f < faces - 1 - me_f, 1, -1)

    def face_at(step):
        near = me_f + (step + 1) // 2 * (-1 if step % 2 else 1)
        return jnp.where(step <= 2 * two_sided, near, me_f + longer * (step - two_sided))

    def px_copy(face, dest, piece, sem, src):
        rows = pl.ds(piece * half, half)
        return pltpu.make_async_remote_copy(
            src_ref=src.at[rows],
            dst_ref=px_all.at[face, rows],
            send_sem=sem,
            recv_sem=px_recv.at[face, piece],
            device_id=(dest, me_s),
            device_id_type=MESH,
        )

    def px_out(piece, side):
        dest = me_f + (1 if side else -1)
        there = (dest >= 0) & (dest < faces)
        return there, px_copy(me_f, dest, piece, px_send.at[0, piece, side], px_ref)

    def px_pass(step, piece):
        face = face_at(step)
        dest = jnp.where(face < me_f, me_f + 1, me_f - 1)
        there = (dest >= 0) & (dest < faces)
        return there, px_copy(face, dest, piece, px_send.at[step, piece, 0], px_all.at[face])

    for piece in range(2):
        for side in range(2):
            there, copy = px_out(piece, side)
            pl.when(there)(copy.start)

    def slab_copy(step, j, r):
        face = face_at(step) if step else me_f
        slab = me_f * n_slab + j
        kind, group = slab // groups, lax.rem(slab, groups)
        dest = group * rep + r
        remote = pltpu.make_async_remote_copy(
            src_ref=proj.at[step, j],
            dst_ref=slabs_ref.at[kind, me_s],
            send_sem=slab_send.at[step, j, r],
            recv_sem=slab_recv.at[kind, me_s],
            device_id=(face, dest),
            device_id_type=MESH,
        )
        local = pltpu.make_async_copy(
            proj.at[step, j], slabs_ref.at[kind, me_s], slab_recv.at[kind, me_s]
        )
        return remote, local, dest

    def gate_copy(step, i, r):
        face = face_at(step) if step else me_f
        first = me_f * gate_cols
        kind, group = first // heads, lax.rem(first, heads) // per_group + i
        dest = group * rep + r
        remote = pltpu.make_async_remote_copy(
            src_ref=glog.at[step],
            dst_ref=gates_ref.at[kind, me_s],
            send_sem=gate_send.at[step, i, r],
            recv_sem=gate_recv.at[kind, me_s],
            device_id=(face, dest),
            device_id_type=MESH,
        )
        local = pltpu.make_async_copy(
            glog.at[step], gates_ref.at[kind, me_s], gate_recv.at[kind, me_s]
        )
        return remote, local, dest

    def launch(copies, step):
        remote, local, dest = copies
        if step == 0:
            pl.when(dest == me_s)(local.start)
            pl.when(dest != me_s)(remote.start)
        else:
            remote.start()

    def drain(copies, step):
        remote, _, dest = copies
        if step == 0:
            pl.when(dest != me_s)(remote.wait_send)
        else:
            remote.wait_send()

    def work_on(step, px):
        logits = lax.dot_general(
            wg_ref[...], px, (((1,), (1,)), ((), ())), preferred_element_type=f32
        )
        glog[step] = logits.astype(bf16).astype(f32)
        whole = jnp.dot(px, weights[...], preferred_element_type=f32).astype(bf16)
        for j in range(n_slab):
            proj[step, j] = whole[:, j * width : (j + 1) * width]

    def send_out(step):
        for i in range(n_gate):
            for r in range(rep):
                launch(gate_copy(step, i, r), step)
        for j in range(n_slab):
            for r in range(rep):
                launch(slab_copy(step, j, r), step)

    fetch.wait()
    work_on(0, px_ref[...])
    send_out(0)
    for step in range(1, faces):
        face = face_at(step)
        for piece in range(2):
            rows = pl.ds(piece * half, half)
            pltpu.make_async_copy(
                px_ref.at[rows], px_all.at[face, rows], px_recv.at[face, piece]
            ).wait()
            there, copy = px_pass(step, piece)
            pl.when(there)(copy.start)
        if step < faces - 1:
            work_on(step, px_all[face])
    for step in range(1, faces - 1):
        send_out(step)
    work_on(faces - 1, px_all[face_at(faces - 1)])
    send_out(faces - 1)

    for piece in range(2):
        for side in range(2):
            there, copy = px_out(piece, side)
            pl.when(there)(copy.wait_send)
        for step in range(1, faces):
            there, copy = px_pass(step, piece)
            pl.when(there)(copy.wait_send)
    for step in range(faces):
        for i in range(n_gate):
            for r in range(rep):
                drain(gate_copy(step, i, r), step)
        for j in range(n_slab):
            for r in range(rep):
                drain(slab_copy(step, j, r), step)
    for source in range(strips):
        for kind in range(slabs_ref.shape[0]):
            pltpu.make_async_copy(
                proj.at[0, 0], slabs_ref.at[kind, source], slab_recv.at[kind, source]
            ).wait()
        for kind in range(gates_ref.shape[0]):
            pltpu.make_async_copy(
                glog.at[0], gates_ref.at[kind, source], gate_recv.at[kind, source]
            ).wait()


def mm(a, b, dims=((1,), (0,))):
    return lax.dot_general(
        a.astype(bf16), b.astype(bf16), (dims, ((), ())), preferred_element_type=f32
    )


def split_mm(exact, wide, pieces):
    exact = exact.astype(bf16)
    total, rest = None, wide
    for _ in range(pieces):
        piece = rest.astype(bf16)
        rest = rest - piece.astype(f32)
        term = jnp.dot(exact, piece, preferred_element_type=f32)
        total = term if total is None else total + term
    return total


def mm_split(wide, exact, pieces):
    exact = exact.astype(bf16)
    total, rest = None, wide
    for _ in range(pieces):
        piece = rest.astype(bf16)
        rest = rest - piece.astype(f32)
        term = jnp.dot(piece, exact, preferred_element_type=f32)
        total = term if total is None else total + term
    return total


def scan_kernel(
    cfg, first_ref, slabs_ref, gates_ref, rate_ref, bias_ref, out_ref,
    feats, gates, row_buf, col_buf, states,
):
    chunk, per_group, tall, wide, dk = cfg
    strips, block, width = slabs_ref.shape[1:]
    count = strips * block
    first = first_ref[0]
    gate_cols = gates_ref.shape[2]

    lane = lax.broadcasted_iota(jnp.int32, (width, width), 1)
    sub = lax.broadcasted_iota(jnp.int32, (width, width), 0)
    same_head = (lane // dk) == (sub // dk)
    head_ones = same_head.astype(f32)
    ti = lax.broadcasted_iota(jnp.int32, (chunk, chunk), 0)
    tj = lax.broadcasted_iota(jnp.int32, (chunk, chunk), 1)
    inclusive = ti >= tj
    tri = inclusive.astype(f32)
    eye = (ti == tj).astype(f32)

    def prepare(s, carry):
        at = pl.ds(s * block, block)
        for kind in range(3):
            x = slabs_ref[kind, s].astype(f32)
            if kind < 2:
                x = x * lax.rsqrt(mm_split(x * x, head_ones, 2) + 1e-06)
            feats[kind, at, :] = x
        for a in range(per_group):
            head = first + a
            row = lax.rem(head, gate_cols)
            decay = -rate_ref[head] * jnp.exp(gates_ref[0, s, pl.ds(row, 1), :])
            strength = jax.nn.sigmoid(gates_ref[1, s, pl.ds(row, 1), :] + bias_ref[head])
            gates[a, at, :] = jnp.broadcast_to(decay, (chunk, block)).T
            gates[per_group + a, at, :] = jnp.broadcast_to(strength, (chunk, block)).T
        return carry

    lax.fori_loop(0, strips, prepare, 0, unroll=True if strips <= 8 else 1)

    columns = chunk // tall
    flane = lax.broadcasted_iota(jnp.int32, (chunk, width), 1) // dk

    def lanes_of(parts):
        out = parts[0][:, :width]
        for a in range(1, per_group):
            out = jnp.where(flane == a, parts[a][:, :width], out)
        return out

    def stacked(x):
        if per_group == 1:
            return x
        return jnp.concatenate(
            [jnp.where(flane == a, x, jnp.zeros_like(x)) for a in range(per_group)], axis=0
        )

    def side_by_side(parts):
        return parts[0] if per_group == 1 else jnp.concatenate(parts, axis=1)

    def load(ref, which, i, by_column):
        if not by_column:
            return ref[which, pl.ds(pl.multiple_of(i * chunk, chunk), chunk), :]
        return jnp.concatenate(
            [ref[which, pl.ds(i * columns + c, tall, stride=wide), :] for c in range(columns)],
            axis=0,
        )

    states[...] = jnp.zeros_like(states)

    per_turn = 2 if (count // chunk) % 2 == 0 else 1
    units = [(m, order, a) for m in range(per_turn) for order in range(2) for a in range(per_group)]

    def advance(turn, carry):
        base = turn * per_turn
        inputs, cums, betas, systems, scores = {}, {}, {}, {}, {}
        for m in range(per_turn):
            for order in range(2):
                inputs[m, order] = [load(feats, kind, base + m, order) for kind in range(3)]
        for unit in units:
            m, order, a = unit
            q, k, _ = inputs[m, order]
            cum = split_mm(tri, load(gates, a, base + m, order), 3)
            beta = load(gates, per_group + a, base + m, order)
            gap = cum - cum.T
            within = jnp.where(inclusive, jnp.exp(jnp.where(inclusive, gap, 0.0)), 0.0)
            k_a = k if per_group == 1 else jnp.where(flane == a, k, 0.0)
            q_a = q if per_group == 1 else jnp.where(flane == a, q, 0.0)
            dots = mm(jnp.concatenate([k_a, q_a], axis=0), k, ((1,), (1,)))
            systems[unit] = within * dots[:chunk] * beta
            scores[unit] = (within * dots[chunk:]).astype(bf16)
            cums[unit] = cum
            betas[unit] = beta

        inverses = {}
        half = 1
        while half < chunk:
            here = ((ti // (2 * half)) == (tj // (2 * half))) & (
                (lax.rem(ti, 2 * half) >= half) & (lax.rem(tj, 2 * half) < half)
            )
            lows = {u: jnp.where(here, systems[u], 0.0) for u in units}
            if half == 1:
                inverses = {u: eye - lows[u] for u in units}
            else:
                firsts = {u: mm(lows[u], inverses[u]) for u in units}
                inverses = {u: inverses[u] - mm(inverses[u], firsts[u]) for u in units}
            half *= 2

        pairs = [(m, order) for m in range(per_turn) for order in range(2)]
        ready = {}
        for m, order in pairs:
            q, k, v = inputs[m, order]
            mine = [(m, order, a) for a in range(per_group)]
            beta = lanes_of([betas[u] for u in mine])
            cum = lanes_of([cums[u] for u in mine])
            scale = jnp.exp(cum)
            last = cum[chunk - 1 : chunk, :]
            both = side_by_side([inverses[u].astype(bf16) for u in mine])
            u_part = mm(both, stacked((v * beta).astype(bf16)))
            w_part = mm(both, stacked((k * (beta * scale)).astype(bf16)))
            keys_out = (k * jnp.exp(last - cum)).astype(bf16)
            reads = side_by_side([scores[u] for u in mine])
            ready[m, order] = (u_part, w_part, q * scale, keys_out, reads, jnp.exp(last))
        for m, order in pairs:
            u_part, w_part, q_part, keys_out, reads, end = ready[m, order]
            i = base + m
            state = states[order]
            fresh = u_part - mm(w_part, state)
            out = mm(q_part, state) + mm(reads, stacked(fresh.astype(bf16)))
            grown = mm(keys_out, fresh, ((0,), (0,)))
            states[order] = state * end + jnp.where(same_head, grown, 0.0)
            normed = out * lax.rsqrt(mm_split(out * out, head_ones, 2) * (1.0 / dk) + 1e-06)
            if order == 0:
                row_buf[pl.ds(pl.multiple_of(i * chunk, chunk), chunk), :] = normed
            else:
                normed = normed.astype(bf16).astype(f32)
                for c in range(columns):
                    col_buf[pl.ds(i * columns + c, tall, stride=wide), :] = normed[
                        c * tall : (c + 1) * tall
                    ]
        return carry

    lax.fori_loop(0, count // chunk // per_turn, advance, 0)

    def finish(s, carry):
        at = pl.ds(s * block, block)
        out_ref[s] = (row_buf[at, :] + col_buf[at, :]).astype(bf16)
        return carry

    lax.fori_loop(0, strips, finish, 0)


def return_kernel(rep, strips, mixed_ref, out_ref, send_sem, recv_sem):
    me_f, me_s = lax.axis_index("face"), lax.axis_index("strip")
    barrier = pltpu.get_barrier_semaphore()
    for step in range(1, strips):
        pl.semaphore_signal(
            barrier, inc=1, device_id=(me_f, lax.rem(me_s + step, strips)), device_id_type=MESH
        )
    pl.semaphore_wait(barrier, strips - 1)

    width = mixed_ref.shape[2]
    mine = me_s // rep

    def place(group):
        if len(out_ref.shape) == 3:
            return out_ref.at[group]
        return out_ref.at[:, pl.ds(pl.multiple_of(group * width, width), width)]

    def copy(step):
        dest = lax.rem(me_s + step, strips)
        return pltpu.make_async_remote_copy(
            src_ref=mixed_ref.at[dest],
            dst_ref=place(mine),
            send_sem=send_sem.at[step],
            recv_sem=recv_sem.at[mine],
            device_id=(me_f, dest),
            device_id_type=MESH,
        )

    @pl.when(lax.rem(me_s, rep) == 0)
    def _():
        for step in range(1, strips):
            copy(step).start()
        pltpu.make_async_copy(mixed_ref.at[me_s], place(mine), recv_sem.at[mine]).start()
        for step in range(1, strips):
            copy(step).wait_send()

    for group in range(strips // rep):
        pltpu.make_async_copy(mixed_ref.at[0], place(group), recv_sem.at[group]).wait()


def scan_call(first, slabs, gates, decay_rate, beta_bias, per_group, tall, wide, dk):
    strips, block, width = slabs.shape[1:]
    count = strips * block
    chunk = min(128, count)
    vmem = pl.BlockSpec(memory_space=pltpu.VMEM)
    smem = pl.BlockSpec(memory_space=pltpu.SMEM)
    return pl.pallas_call(
        functools.partial(scan_kernel, (chunk, per_group, tall, wide, dk)),
        out_shape=jax.ShapeDtypeStruct((strips, block, width), bf16),
        in_specs=[smem, vmem, vmem, smem, smem],
        out_specs=vmem,
        scratch_shapes=[
            pltpu.VMEM((3, count, width), f32),
            pltpu.VMEM((2 * per_group, count, chunk), f32),
            pltpu.VMEM((count, width), f32),
            pltpu.VMEM((count, width), f32),
            pltpu.VMEM((2, width, width), f32),
        ],
        name="scans",
    )(first, slabs, gates, decay_rate, beta_bias)


def on_device(faces, strips, pixels_in, w_qkv, w_gate, decay_rate, beta_bias):
    _, rows_here, wide, features = pixels_in.shape
    heads = decay_rate.shape[0]
    block = rows_here * wide
    tall = rows_here * strips
    model = w_qkv.shape[1] * faces // 3
    dk = model // heads
    groups = min(strips, heads)
    rep = strips // groups
    per_group = heads // groups
    width = per_group * dk
    n_slab = w_qkv.shape[1] // width
    gate_cols = w_gate.shape[1]
    n_gate = gate_cols // per_group
    vmem = pl.BlockSpec(memory_space=pltpu.VMEM)
    dma = pltpu.SemaphoreType.DMA
    slabs, gates = pl.pallas_call(
        functools.partial(project_kernel, (faces, strips, groups, rep, heads, per_group)),
        out_shape=(
            jax.ShapeDtypeStruct((3, strips, block, width), bf16),
            jax.ShapeDtypeStruct((2, strips, gate_cols, block), f32),
        ),
        in_specs=[vmem, pl.BlockSpec(memory_space=pl.ANY), vmem],
        out_specs=(vmem, vmem),
        scratch_shapes=[
            pltpu.VMEM((faces, block, features), bf16),
            pltpu.VMEM((faces, n_slab, block, width), bf16),
            pltpu.VMEM((faces, gate_cols, block), f32),
            pltpu.VMEM(w_qkv.shape, bf16),
            dma(()),
            dma((faces, 2, 2)),
            dma((faces, 2)),
            dma((faces, n_slab, rep)),
            dma((3, strips)),
            dma((faces, n_gate, rep)),
            dma((2, strips)),
        ],
        compiler_params=pltpu.CompilerParams(collective_id=0, has_side_effects=True),
        name="project",
    )(pixels_in.reshape(block, features), w_qkv, w_gate.T)
    first = (lax.axis_index("strip") // rep * per_group).astype(jnp.int32).reshape(1)
    mixed = scan_call(first, slabs, gates, decay_rate, beta_bias, per_group, tall, wide, dk)
    flat = width % 128 == 0
    returned = pl.pallas_call(
        functools.partial(return_kernel, rep, strips),
        out_shape=jax.ShapeDtypeStruct(
            (block, model) if flat else (groups, block, width), bf16
        ),
        in_specs=[vmem],
        out_specs=vmem,
        scratch_shapes=[dma((strips,)), dma((groups,))],
        compiler_params=pltpu.CompilerParams(collective_id=1, has_side_effects=True),
        name="give_back",
    )(mixed)
    if not flat:
        returned = returned.transpose(1, 0, 2)
    return returned.reshape(1, rows_here, wide, model)


def solution(mesh):
    in_specs = (P("face", "strip", None, None), P(None, "face"), P(None, "face"), P(), P())
    out_specs = P("face", "strip", None, None)
    return jax.shard_map(
        functools.partial(on_device, mesh.shape["face"], mesh.shape["strip"]),
        mesh=mesh,
        in_specs=in_specs,
        out_specs=out_specs,
        check_vma=False,
    )
```

```python
import functools

import jax
import jax.numpy as jnp
from jax import lax
from jax.experimental import pallas as pl
from jax.experimental.pallas import tpu as pltpu
from jax.sharding import PartitionSpec as P

MESH = pl.DeviceIdType.MESH
f32 = jnp.float32
bf16 = jnp.bfloat16


def greet_all(faces, strips, me_f, me_s):
    barrier = pltpu.get_barrier_semaphore()
    total = faces * strips
    me = me_f * strips + me_s

    def one(step, carry):
        other = lax.rem(me + step, total)
        pl.semaphore_signal(
            barrier,
            inc=1,
            device_id=(other // strips, lax.rem(other, strips)),
            device_id_type=MESH,
        )
        return carry

    lax.fori_loop(1, total, one, 0)
    pl.semaphore_wait(barrier, total - 1)


def project_kernel(
    cfg, px_ref, wq_ref, wg_ref, slabs_ref, gates_ref,
    px_all, proj, glog, weights, weight_sem, px_send, px_recv, slab_send, slab_recv, gate_send, gate_recv,
):
    faces, strips, groups, rep, heads, per_group = cfg
    me_f, me_s = lax.axis_index("face"), lax.axis_index("strip")
    n_slab = proj.shape[1]
    gate_cols = wg_ref.shape[0]
    width = proj.shape[3]
    n_gate = gate_cols // per_group
    block = px_ref.shape[0]
    half = block // 2
    fetch = pltpu.make_async_copy(wq_ref, weights, weight_sem)
    fetch.start()
    greet_all(faces, strips, me_f, me_s)
    two_sided = jnp.minimum(me_f, faces - 1 - me_f)
    longer = jnp.where(me_f < faces - 1 - me_f, 1, -1)

    def face_at(step):
        near = me_f + (step + 1) // 2 * (-1 if step % 2 else 1)
        return jnp.where(step <= 2 * two_sided, near, me_f + longer * (step - two_sided))

    def px_copy(face, dest, piece, sem, src):
        rows = pl.ds(piece * half, half)
        return pltpu.make_async_remote_copy(
            src_ref=src.at[rows],
            dst_ref=px_all.at[face, rows],
            send_sem=sem,
            recv_sem=px_recv.at[face, piece],
            device_id=(dest, me_s),
            device_id_type=MESH,
        )

    def px_out(piece, side):
        dest = me_f + (1 if side else -1)
        there = (dest >= 0) & (dest < faces)
        return there, px_copy(me_f, dest, piece, px_send.at[0, piece, side], px_ref)

    def px_pass(step, piece):
        face = face_at(step)
        dest = jnp.where(face < me_f, me_f + 1, me_f - 1)
        there = (dest >= 0) & (dest < faces)
        return there, px_copy(face, dest, piece, px_send.at[step, piece, 0], px_all.at[face])

    for piece in range(2):
        for side in range(2):
            there, copy = px_out(piece, side)
            pl.when(there)(copy.start)

    def slab_copy(step, j, r):
        face = face_at(step) if step else me_f
        slab = me_f * n_slab + j
        kind, group = slab // groups, lax.rem(slab, groups)
        dest = group * rep + r
        remote = pltpu.make_async_remote_copy(
            src_ref=proj.at[step, j],
            dst_ref=slabs_ref.at[kind, me_s],
            send_sem=slab_send.at[step, j, r],
            recv_sem=slab_recv.at[kind, me_s],
            device_id=(face, dest),
            device_id_type=MESH,
        )
        local = pltpu.make_async_copy(
            proj.at[step, j], slabs_ref.at[kind, me_s], slab_recv.at[kind, me_s]
        )
        return remote, local, dest

    def gate_copy(step, i, r):
        face = face_at(step) if step else me_f
        first = me_f * gate_cols
        kind, group = first // heads, lax.rem(first, heads) // per_group + i
        dest = group * rep + r
        remote = pltpu.make_async_remote_copy(
            src_ref=glog.at[step],
            dst_ref=gates_ref.at[kind, me_s],
            send_sem=gate_send.at[step, i, r],
            recv_sem=gate_recv.at[kind, me_s],
            device_id=(face, dest),
            device_id_type=MESH,
        )
        local = pltpu.make_async_copy(
            glog.at[step], gates_ref.at[kind, me_s], gate_recv.at[kind, me_s]
        )
        return remote, local, dest

    def launch(copies, step):
        remote, local, dest = copies
        if step == 0:
            pl.when(dest == me_s)(local.start)
            pl.when(dest != me_s)(remote.start)
        else:
            remote.start()

    def drain(copies, step):
        remote, _, dest = copies
        if step == 0:
            pl.when(dest != me_s)(remote.wait_send)
        else:
            remote.wait_send()

    def work_on(step, px):
        logits = lax.dot_general(
            wg_ref[...], px, (((1,), (1,)), ((), ())), preferred_element_type=f32
        )
        glog[step] = logits.astype(bf16).astype(f32)
        whole = jnp.dot(px, weights[...], preferred_element_type=f32).astype(bf16)
        for j in range(n_slab):
            proj[step, j] = whole[:, j * width : (j + 1) * width]

    def send_out(step):
        for i in range(n_gate):
            for r in range(rep):
                launch(gate_copy(step, i, r), step)
        for j in range(n_slab):
            for r in range(rep):
                launch(slab_copy(step, j, r), step)

    fetch.wait()
    work_on(0, px_ref[...])
    send_out(0)
    for step in range(1, faces):
        face = face_at(step)
        for piece in range(2):
            rows = pl.ds(piece * half, half)
            pltpu.make_async_copy(
                px_ref.at[rows], px_all.at[face, rows], px_recv.at[face, piece]
            ).wait()
            there, copy = px_pass(step, piece)
            pl.when(there)(copy.start)
        if step < faces - 1:
            work_on(step, px_all[face])
    for step in range(1, faces - 1):
        send_out(step)
    work_on(faces - 1, px_all[face_at(faces - 1)])
    send_out(faces - 1)

    for piece in range(2):
        for side in range(2):
            there, copy = px_out(piece, side)
            pl.when(there)(copy.wait_send)
        for step in range(1, faces):
            there, copy = px_pass(step, piece)
            pl.when(there)(copy.wait_send)
    for step in range(faces):
        for i in range(n_gate):
            for r in range(rep):
                drain(gate_copy(step, i, r), step)
        for j in range(n_slab):
            for r in range(rep):
                drain(slab_copy(step, j, r), step)
    for source in range(strips):
        for kind in range(slabs_ref.shape[0]):
            pltpu.make_async_copy(
                proj.at[0, 0], slabs_ref.at[kind, source], slab_recv.at[kind, source]
            ).wait()
        for kind in range(gates_ref.shape[0]):
            pltpu.make_async_copy(
                glog.at[0], gates_ref.at[kind, source], gate_recv.at[kind, source]
            ).wait()


def mm(a, b, dims=((1,), (0,))):
    return lax.dot_general(
        a.astype(bf16), b.astype(bf16), (dims, ((), ())), preferred_element_type=f32
    )


def split_mm(exact, wide, pieces):
    exact = exact.astype(bf16)
    total, rest = None, wide
    for _ in range(pieces):
        piece = rest.astype(bf16)
        rest = rest - piece.astype(f32)
        term = jnp.dot(exact, piece, preferred_element_type=f32)
        total = term if total is None else total + term
    return total


def mm_split(wide, exact, pieces):
    exact = exact.astype(bf16)
    total, rest = None, wide
    for _ in range(pieces):
        piece = rest.astype(bf16)
        rest = rest - piece.astype(f32)
        term = jnp.dot(piece, exact, preferred_element_type=f32)
        total = term if total is None else total + term
    return total


def scan_kernel(
    cfg, first_ref, slabs_ref, gates_ref, rate_ref, bias_ref, out_ref,
    feats, gates, row_buf, col_buf, states,
):
    chunk, per_group, tall, wide, dk = cfg
    strips, block, width = slabs_ref.shape[1:]
    count = strips * block
    first = first_ref[0]
    gate_cols = gates_ref.shape[2]

    lane = lax.broadcasted_iota(jnp.int32, (width, width), 1)
    sub = lax.broadcasted_iota(jnp.int32, (width, width), 0)
    same_head = (lane // dk) == (sub // dk)
    head_ones = same_head.astype(f32)
    ti = lax.broadcasted_iota(jnp.int32, (chunk, chunk), 0)
    tj = lax.broadcasted_iota(jnp.int32, (chunk, chunk), 1)
    inclusive = ti >= tj
    tri = inclusive.astype(f32)
    eye = (ti == tj).astype(f32)

    def prepare(s, carry):
        at = pl.ds(s * block, block)
        for kind in range(3):
            x = slabs_ref[kind, s].astype(f32)
            if kind < 2:
                x = x * lax.rsqrt(mm_split(x * x, head_ones, 2) + 1e-06)
            feats[kind, at, :] = x
        for a in range(per_group):
            head = first + a
            row = lax.rem(head, gate_cols)
            decay = -rate_ref[head] * jnp.exp(gates_ref[0, s, pl.ds(row, 1), :])
            strength = jax.nn.sigmoid(gates_ref[1, s, pl.ds(row, 1), :] + bias_ref[head])
            gates[a, at, :] = jnp.broadcast_to(decay, (chunk, block)).T
            gates[per_group + a, at, :] = jnp.broadcast_to(strength, (chunk, block)).T
        return carry

    lax.fori_loop(0, strips, prepare, 0, unroll=True if strips <= 8 else 1)

    columns = chunk // tall
    flane = lax.broadcasted_iota(jnp.int32, (chunk, width), 1) // dk

    def lanes_of(parts):
        out = parts[0][:, :width]
        for a in range(1, per_group):
            out = jnp.where(flane == a, parts[a][:, :width], out)
        return out

    def stacked(x):
        if per_group == 1:
            return x
        return jnp.concatenate(
            [jnp.where(flane == a, x, jnp.zeros_like(x)) for a in range(per_group)], axis=0
        )

    def side_by_side(parts):
        return parts[0] if per_group == 1 else jnp.concatenate(parts, axis=1)

    def load(ref, which, i, by_column):
        if not by_column:
            return ref[which, pl.ds(pl.multiple_of(i * chunk, chunk), chunk), :]
        return jnp.concatenate(
            [ref[which, pl.ds(i * columns + c, tall, stride=wide), :] for c in range(columns)],
            axis=0,
        )

    states[...] = jnp.zeros_like(states)

    per_turn = 4 if count // chunk == 4 else (2 if (count // chunk) % 2 == 0 else 1)
    units = [(m, order, a) for m in range(per_turn) for order in range(2) for a in range(per_group)]

    def advance(turn, carry):
        base = turn * per_turn
        inputs, cums, betas, systems, scores = {}, {}, {}, {}, {}
        for m in range(per_turn):
            for order in range(2):
                inputs[m, order] = [load(feats, kind, base + m, order) for kind in range(3)]
        for unit in units:
            m, order, a = unit
            q, k, _ = inputs[m, order]
            cum = split_mm(tri, load(gates, a, base + m, order), 3)
            beta = load(gates, per_group + a, base + m, order)
            gap = cum - cum.T
            within = jnp.where(inclusive, jnp.exp(jnp.where(inclusive, gap, 0.0)), 0.0)
            k_a = k if per_group == 1 else jnp.where(flane == a, k, 0.0)
            q_a = q if per_group == 1 else jnp.where(flane == a, q, 0.0)
            dots = mm(jnp.concatenate([k_a, q_a], axis=0), k, ((1,), (1,)))
            systems[unit] = within * dots[:chunk] * beta
            scores[unit] = (within * dots[chunk:]).astype(bf16)
            cums[unit] = cum
            betas[unit] = beta

        inverses = {}
        half = 1
        while half < chunk:
            here = ((ti // (2 * half)) == (tj // (2 * half))) & (
                (lax.rem(ti, 2 * half) >= half) & (lax.rem(tj, 2 * half) < half)
            )
            lows = {u: jnp.where(here, systems[u], 0.0) for u in units}
            if half == 1:
                inverses = {u: eye - lows[u] for u in units}
            else:
                firsts = {u: mm(lows[u], inverses[u]) for u in units}
                inverses = {u: inverses[u] - mm(inverses[u], firsts[u]) for u in units}
            half *= 2

        pairs = [(m, order) for m in range(per_turn) for order in range(2)]
        ready = {}
        for m, order in pairs:
            q, k, v = inputs[m, order]
            mine = [(m, order, a) for a in range(per_group)]
            beta = lanes_of([betas[u] for u in mine])
            cum = lanes_of([cums[u] for u in mine])
            scale = jnp.exp(cum)
            last = cum[chunk - 1 : chunk, :]
            both = side_by_side([inverses[u].astype(bf16) for u in mine])
            u_part = mm(both, stacked((v * beta).astype(bf16)))
            w_part = mm(both, stacked((k * (beta * scale)).astype(bf16)))
            keys_out = (k * jnp.exp(last - cum)).astype(bf16)
            reads = side_by_side([scores[u] for u in mine])
            ready[m, order] = (u_part, w_part, q * scale, keys_out, reads, jnp.exp(last))
        for m, order in pairs:
            u_part, w_part, q_part, keys_out, reads, end = ready[m, order]
            i = base + m
            state = states[order]
            fresh = u_part - mm(w_part, state)
            out = mm(q_part, state) + mm(reads, stacked(fresh.astype(bf16)))
            grown = mm(keys_out, fresh, ((0,), (0,)))
            states[order] = state * end + jnp.where(same_head, grown, 0.0)
            normed = out * lax.rsqrt(mm_split(out * out, head_ones, 2) * (1.0 / dk) + 1e-06)
            if order == 0:
                row_buf[pl.ds(pl.multiple_of(i * chunk, chunk), chunk), :] = normed
            else:
                normed = normed.astype(bf16).astype(f32)
                for c in range(columns):
                    col_buf[pl.ds(i * columns + c, tall, stride=wide), :] = normed[
                        c * tall : (c + 1) * tall
                    ]
        return carry

    lax.fori_loop(0, count // chunk // per_turn, advance, 0)

    def finish(s, carry):
        at = pl.ds(s * block, block)
        out_ref[s] = (row_buf[at, :] + col_buf[at, :]).astype(bf16)
        return carry

    lax.fori_loop(0, strips, finish, 0)


def return_kernel(rep, strips, mixed_ref, out_ref, send_sem, recv_sem):
    me_f, me_s = lax.axis_index("face"), lax.axis_index("strip")
    barrier = pltpu.get_barrier_semaphore()
    for step in range(1, strips):
        pl.semaphore_signal(
            barrier, inc=1, device_id=(me_f, lax.rem(me_s + step, strips)), device_id_type=MESH
        )
    pl.semaphore_wait(barrier, strips - 1)

    width = mixed_ref.shape[2]
    mine = me_s // rep

    def place(group):
        if len(out_ref.shape) == 3:
            return out_ref.at[group]
        return out_ref.at[:, pl.ds(pl.multiple_of(group * width, width), width)]

    def copy(step):
        dest = lax.rem(me_s + step, strips)
        return pltpu.make_async_remote_copy(
            src_ref=mixed_ref.at[dest],
            dst_ref=place(mine),
            send_sem=send_sem.at[step],
            recv_sem=recv_sem.at[mine],
            device_id=(me_f, dest),
            device_id_type=MESH,
        )

    @pl.when(lax.rem(me_s, rep) == 0)
    def _():
        for step in range(1, strips):
            copy(step).start()
        pltpu.make_async_copy(mixed_ref.at[me_s], place(mine), recv_sem.at[mine]).start()
        for step in range(1, strips):
            copy(step).wait_send()

    for group in range(strips // rep):
        pltpu.make_async_copy(mixed_ref.at[0], place(group), recv_sem.at[group]).wait()


def scan_call(first, slabs, gates, decay_rate, beta_bias, per_group, tall, wide, dk):
    strips, block, width = slabs.shape[1:]
    count = strips * block
    chunk = min(128, count)
    vmem = pl.BlockSpec(memory_space=pltpu.VMEM)
    smem = pl.BlockSpec(memory_space=pltpu.SMEM)
    return pl.pallas_call(
        functools.partial(scan_kernel, (chunk, per_group, tall, wide, dk)),
        out_shape=jax.ShapeDtypeStruct((strips, block, width), bf16),
        in_specs=[smem, vmem, vmem, smem, smem],
        out_specs=vmem,
        scratch_shapes=[
            pltpu.VMEM((3, count, width), f32),
            pltpu.VMEM((2 * per_group, count, chunk), f32),
            pltpu.VMEM((count, width), f32),
            pltpu.VMEM((count, width), f32),
            pltpu.VMEM((2, width, width), f32),
        ],
        name="scans",
    )(first, slabs, gates, decay_rate, beta_bias)


def on_device(faces, strips, pixels_in, w_qkv, w_gate, decay_rate, beta_bias):
    _, rows_here, wide, features = pixels_in.shape
    heads = decay_rate.shape[0]
    block = rows_here * wide
    tall = rows_here * strips
    model = w_qkv.shape[1] * faces // 3
    dk = model // heads
    groups = min(strips, heads)
    rep = strips // groups
    per_group = heads // groups
    width = per_group * dk
    n_slab = w_qkv.shape[1] // width
    gate_cols = w_gate.shape[1]
    n_gate = gate_cols // per_group
    vmem = pl.BlockSpec(memory_space=pltpu.VMEM)
    dma = pltpu.SemaphoreType.DMA
    slabs, gates = pl.pallas_call(
        functools.partial(project_kernel, (faces, strips, groups, rep, heads, per_group)),
        out_shape=(
            jax.ShapeDtypeStruct((3, strips, block, width), bf16),
            jax.ShapeDtypeStruct((2, strips, gate_cols, block), f32),
        ),
        in_specs=[vmem, pl.BlockSpec(memory_space=pl.ANY), vmem],
        out_specs=(vmem, vmem),
        scratch_shapes=[
            pltpu.VMEM((faces, block, features), bf16),
            pltpu.VMEM((faces, n_slab, block, width), bf16),
            pltpu.VMEM((faces, gate_cols, block), f32),
            pltpu.VMEM(w_qkv.shape, bf16),
            dma(()),
            dma((faces, 2, 2)),
            dma((faces, 2)),
            dma((faces, n_slab, rep)),
            dma((3, strips)),
            dma((faces, n_gate, rep)),
            dma((2, strips)),
        ],
        compiler_params=pltpu.CompilerParams(collective_id=0, has_side_effects=True),
        name="project",
    )(pixels_in.reshape(block, features), w_qkv, w_gate.T)
    first = (lax.axis_index("strip") // rep * per_group).astype(jnp.int32).reshape(1)
    mixed = scan_call(first, slabs, gates, decay_rate, beta_bias, per_group, tall, wide, dk)
    flat = width % 128 == 0
    returned = pl.pallas_call(
        functools.partial(return_kernel, rep, strips),
        out_shape=jax.ShapeDtypeStruct(
            (block, model) if flat else (groups, block, width), bf16
        ),
        in_specs=[vmem],
        out_specs=vmem,
        scratch_shapes=[dma((strips,)), dma((groups,))],
        compiler_params=pltpu.CompilerParams(collective_id=1, has_side_effects=True),
        name="give_back",
    )(mixed)
    if not flat:
        returned = returned.transpose(1, 0, 2)
    return returned.reshape(1, rows_here, wide, model)


def solution(mesh):
    in_specs = (P("face", "strip", None, None), P(None, "face"), P(None, "face"), P(), P())
    out_specs = P("face", "strip", None, None)
    return jax.shard_map(
        functools.partial(on_device, mesh.shape["face"], mesh.shape["strip"]),
        mesh=mesh,
        in_specs=in_specs,
        out_specs=out_specs,
        check_vma=False,
    )
```
